768 devices in a mesh: seq: 12 (over z), tensor: 64 (over x, y, core).
Axes of the slice: x: 4, y: 8, z: 12, core: 2. Of those that a mesh axis runs over, the one named last changes fastest.
Arguments:
- layer_inputs: bfloat16 [2304, 6144], P('seq'), may hold values from -16 to 16
- projection_matrices: bfloat16 [6144, 3, 6144], P(None, None, 'tensor'), may hold values from -0.21875 to 0.21875
- result_sensitivity: bfloat16 [2304, 6144], P('seq', 'tensor'), may hold values from -4.5 to 4.5
- channel_fading_rate: float32 [64], P('tensor'), may hold values from 8.680556e-06 to 0.03
- loss_events: int32 [4], replicated, may hold values from 0 to 2303
Outputs:
- input_grad: bfloat16 [6144, 2304], P('tensor', 'seq')
- weight_grad: bfloat16 [6144, 3, 6144], P('seq', None, 'tensor')
The draws below stay inside these ranges and needn't reach their ends.
All inputs are finite; a program needn't handle non-finite values.
Results may differ from the reference program's by a relative error of at most 0.023.
Values may be sent and summed in bfloat16 or wider, within the bound.
No kernel may reach another device: no remote copies, remote signals or barrier semaphores. Data moves between devices by JAX's collectives and lax.ppermute only.
A program may use at most 64 MiB of HBM per device.

```python
import math
import jax
import jax.numpy as jnp
from jax import lax

D = 6144
DH = 96
TOK_DEV = 192
MEMORY_LOSSES = 4
HEADS = 64
SEQUENCE_LENGTH = 2304
N_SEQ = 12


SPIKE_FACTOR = 4.0


INPUT_LIMIT = 16.0


SENSITIVITY_LIMIT = 4.5


def draw_channel_fading_rate(key, part):
    lower = math.log(0.02 / SEQUENCE_LENGTH)
    upper = math.log(0.03)
    spread = jax.random.uniform(key, (HEADS,), jnp.float32, lower, upper)
    return jnp.exp(spread)


def draw_layer_inputs(key, part):
    noise_key = jax.random.fold_in(key, 11)
    common_key = jax.random.fold_in(key, 12)
    pair_key = jax.random.fold_in(key, 13)
    rows = jnp.arange(SEQUENCE_LENGTH, dtype=jnp.int32)
    shard = rows // TOK_DEV
    signs = 1.0 - 2.0 * (shard % 2).astype(jnp.float32)
    common = jax.random.normal(common_key, (D,), jnp.float32)
    noise = jax.random.normal(noise_key, (SEQUENCE_LENGTH, D), jnp.float32)
    base = signs[:, None] * common[None, :] + noise
    pairing = jax.random.permutation(pair_key, N_SEQ).astype(jnp.int32)
    column_block = jnp.arange(D, dtype=jnp.int32) // (D // N_SEQ)
    paired = pairing[shard]
    marked = paired[:, None] == column_block[None, :]
    values = jnp.where(marked, SPIKE_FACTOR * base, base)
    return jnp.clip(values, -INPUT_LIMIT, INPUT_LIMIT).astype(jnp.bfloat16)


def draw_result_sensitivity(key, part):
    noise_key = jax.random.fold_in(key, 21)
    common_key = jax.random.fold_in(key, 22)
    common = jax.random.normal(common_key, (HEADS * DH,), jnp.float32)
    noise = jax.random.normal(noise_key, (SEQUENCE_LENGTH, HEADS * DH), jnp.float32)
    values = common[None, :] + noise
    return jnp.clip(values, -SENSITIVITY_LIMIT, SENSITIVITY_LIMIT).astype(jnp.bfloat16)


def plant(drawn, stream_key, low, largest):
    index_at = [jax.random.randint(jax.random.fold_in(stream_key, axis), (), 0, length) for axis, length in enumerate(drawn.shape)]
    longest = drawn.shape.index(max(drawn.shape))
    next_to = index_at[:longest] + [(index_at[longest] + 1) % drawn.shape[longest]] + index_at[longest + 1:]
    return drawn.at[tuple(index_at)].set(low).at[tuple(next_to)].set(largest)


def with_spikes(entries, stream_key, source, target, shards_of, factor):
    def block_of(position):
        return (jnp.arange(entries.shape[position]) // (entries.shape[position] // shards_of)).reshape((-1,) + (1,) * (entries.ndim - 1 - position))

    near = jax.random.permutation(stream_key, shards_of)[block_of(target)]
    other_side = (block_of(target) + shards_of // 2) % shards_of
    return jnp.where((block_of(source) == near) | (block_of(source) == other_side), factor * entries, entries)


def shard_levels(stream_key, shape, pieces, least, top_value):
    level, own = 1.0, jax.random.fold_in(stream_key, 6)
    for dim, parts in pieces:
        steps = jnp.exp(jax.random.uniform(jax.random.fold_in(own, dim), (parts,), jnp.float32, least / len(pieces), top_value / len(pieces)))
        level = level * jnp.repeat(steps, shape[dim] // parts).reshape([-1 if axis == dim else 1 for axis in range(len(shape))])
    return level


def heavy_noise(own_key, dims, scale, most, pieces, heavy, kind=jnp.bfloat16):
    values = scale * jax.random.normal(own_key, dims, jnp.float32)
    if pieces:
        values = values * shard_levels(own_key, dims, pieces, -0.22, 0.18)
    return jnp.clip(with_spikes(values, jax.random.fold_in(own_key, 3), *heavy), -most, most).astype(kind)


def setup_inputs(seed: int = 0) -> dict:
    key_of = jax.random.split(jax.random.key(seed), 6)
    return {
        "layer_inputs": draw_layer_inputs(jax.random.fold_in(key_of[5], 71), 0),
        "projection_matrices": heavy_noise(key_of[1], (D, 3, HEADS * DH), D ** -0.5, 0.21875, ((2, 64),), (2, 0, 64, 4.0)),
        "result_sensitivity": draw_result_sensitivity(jax.random.fold_in(key_of[5], 71), 0),
        "channel_fading_rate": draw_channel_fading_rate(jax.random.fold_in(key_of[5], 71), 0),
        "loss_events": plant(jax.random.randint(key_of[4], (MEMORY_LOSSES,), 0, SEQUENCE_LENGTH), jax.random.fold_in(key_of[4], 1), 0, SEQUENCE_LENGTH - 1).astype(jnp.int32),
    }


DROP_LOGARITHM = 0.3
CLIP_RMS = 0.5

def head_grads(operands):
    query, keys, values, grads_out, logarithm_values = operands
    cumul = jnp.cumsum(logarithm_values)
    length = query.shape[0]
    later = jnp.arange(length)[:, None] >= jnp.arange(length)[None, :]
    weight = jnp.exp(jnp.where(later, cumul[:, None] - cumul[None, :], -jnp.inf))
    highest = lax.Precision.HIGHEST
    scores = jnp.dot(query, keys.T, precision=highest) * weight
    dscores = jnp.dot(grads_out, values.T, precision=highest) * weight
    dquery = jnp.dot(dscores, keys, precision=highest)
    dkey = jnp.dot(dscores.T, query, precision=highest)
    dvalue = jnp.dot(scores.T, grads_out, precision=highest)
    return (dquery, dkey, dvalue)

def reference(layer_inputs, projection_matrices, result_sensitivity, channel_fading_rate, loss_events):
    scale = DH ** (-0.5)
    width = HEADS * DH
    flat_w = projection_matrices.reshape(D, 3 * width)
    proj = jnp.dot(layer_inputs, flat_w, preferred_element_type=jnp.float32).reshape(SEQUENCE_LENGTH, 3, HEADS, DH)
    query = (proj[:, 0] * scale).astype(jnp.bfloat16).astype(jnp.float32).transpose(1, 0, 2)
    keys = proj[:, 1].astype(jnp.bfloat16).astype(jnp.float32).transpose(1, 0, 2)
    values = proj[:, 2].astype(jnp.bfloat16).astype(jnp.float32).transpose(1, 0, 2)
    grads_out = result_sensitivity.reshape(SEQUENCE_LENGTH, HEADS, DH).astype(jnp.float32).transpose(1, 0, 2)
    element_location = jnp.arange(SEQUENCE_LENGTH, dtype=jnp.int32)
    memory_loss_sites = lax.optimization_barrier(jnp.sum((loss_events[None, :] == element_location[:, None]).astype(jnp.float32), axis=1))
    logarithm_values = -(channel_fading_rate[:, None] + DROP_LOGARITHM * memory_loss_sites[None, :])
    dquery, dkey, dvalue = lax.map(head_grads, (query, keys, values, grads_out, logarithm_values))
    stacked = jnp.stack([dquery * scale, dkey, dvalue]).astype(jnp.bfloat16)
    gflat = stacked.transpose(2, 0, 1, 3).reshape(SEQUENCE_LENGTH, 3 * width)
    input_grad = jnp.dot(flat_w, gflat.T, preferred_element_type=jnp.float32).astype(jnp.bfloat16)
    token_blocks = layer_inputs.reshape(N_SEQ, TOK_DEV, D)
    grad_blocks = gflat.reshape(N_SEQ, TOK_DEV, 3 * width)

    def add_block(total, pair):
        block_term = jnp.dot(pair[0].T, pair[1], preferred_element_type=jnp.float32)
        rounded = lax.optimization_barrier(block_term.astype(jnp.bfloat16))
        return (total + rounded.astype(jnp.float32), None)
    summed, _ = lax.scan(add_block, jnp.zeros((D, 3 * width), jnp.float32), (token_blocks, grad_blocks))
    square = jnp.sum(summed * summed)
    factor = jnp.minimum(1.0, CLIP_RMS * math.sqrt(D * 3 * width) / jnp.sqrt(square + 1e-06))
    weight_grad = (summed * factor).astype(jnp.bfloat16).reshape(D, 3, width)
    return (input_grad, weight_grad)
```

```python
import math

import jax
import jax.numpy as jnp
from jax import lax
from jax.sharding import Mesh, PartitionSpec as P

DH = 96
N_SEQ = 12
NX, NY, NC = 4, 8, 2

DROP_LOGARITHM = 0.3
CLIP_RMS = 0.5
EXACT = lax.Precision.HIGHEST
F32 = jnp.float32
BF16 = jnp.bfloat16
TENSOR = ("x", "y", "core")


def body(layer_inputs, projection_matrices, result_sensitivity, channel_fading_rate, loss_events):
    row_count, width = layer_inputs.shape
    scale = DH ** (-0.5)
    me = lax.axis_index("seq")
    proj = jnp.einsum("td,dpe->pte", layer_inputs, projection_matrices, preferred_element_type=F32)
    query = (proj[0] * scale).astype(BF16)
    keys = proj[1].astype(BF16)
    values = proj[2].astype(BF16)
    rate = channel_fading_rate[0]

    steps = jnp.arange(row_count, dtype=jnp.int32)
    place = loss_events - me * row_count
    seen = jnp.sum(((place[None, :] <= steps[:, None]) & (place[None, :] >= 0)).astype(F32), axis=1)
    cumul = -(rate * (steps + 1).astype(F32) + DROP_LOGARITHM * seen)
    shards = jnp.arange(N_SEQ, dtype=jnp.int32)
    events_of = jnp.sum((loss_events[None, :] // row_count == shards[:, None]).astype(F32), axis=1)
    totals = -(rate * row_count + DROP_LOGARITHM * events_of)
    mine_total = jnp.sum(jnp.where(shards == me, totals, 0.0))
    low = jnp.minimum(shards, me)[:, None]
    high = jnp.maximum(shards, me)[:, None]
    between = (shards[None, :] > low) & (shards[None, :] < high)
    hop_w = jnp.exp(jnp.sum(jnp.where(between, totals[None, :], 0.0), axis=1))
    tail_w = jnp.exp(mine_total - cumul)
    head_w = jnp.exp(cumul)

    q32, k32, v32, o32 = (a.astype(F32) for a in (query, keys, values, result_sensitivity))
    fwd_state = jnp.einsum("sf,se->fe", v32 * tail_w[:, None], k32, precision=EXACT)
    rev_state = jnp.einsum("te,tf->ef", q32 * head_w[:, None], o32, precision=EXACT)
    to_later = (shards > me)[:, None, None]
    to_send = hop_w[:, None, None] * jnp.where(to_later, fwd_state[None], rev_state[None])
    got = lax.all_to_all(to_send.astype(BF16), "seq", 0, 0, tiled=True).astype(F32)
    prefix = jnp.sum(jnp.where((shards < me)[:, None, None], got, 0.0), axis=0)
    suffix = jnp.sum(jnp.where((shards > me)[:, None, None], got, 0.0), axis=0)

    later = steps[:, None] >= steps[None, :]
    weight = jnp.exp(jnp.where(later, cumul[:, None] - cumul[None, :], -jnp.inf))
    scores = jnp.einsum("te,se->ts", query, keys, preferred_element_type=F32) * weight
    dscores = jnp.einsum("tf,sf->ts", result_sensitivity, values, preferred_element_type=F32) * weight
    dquery = jnp.einsum("ts,se->te", dscores, k32, precision=EXACT) + head_w[:, None] * jnp.einsum(
        "tf,fe->te", o32, prefix, precision=EXACT
    )
    dkey = jnp.einsum("ts,te->se", dscores, q32, precision=EXACT) + tail_w[:, None] * jnp.einsum(
        "sf,ef->se", v32, suffix, precision=EXACT
    )
    dvalue = jnp.einsum("ts,tf->sf", scores, o32, precision=EXACT) + tail_w[:, None] * jnp.einsum(
        "se,ef->sf", k32, suffix, precision=EXACT
    )
    grads = jnp.stack([dquery * scale, dkey, dvalue]).astype(BF16)

    terms = jnp.einsum("tr,pte->rpe", layer_inputs, grads, preferred_element_type=F32).astype(BF16)
    summed = lax.psum_scatter(terms, "seq", scatter_dimension=0, tiled=True)

    part = jnp.einsum("rpe,pte->rt", projection_matrices, grads, preferred_element_type=F32)
    part = part.reshape(NX, NY, NC, width // (NX * NY * NC), row_count)
    core = lax.axis_index("core")
    keep = lax.dynamic_index_in_dim(part, core, 2, keepdims=False)
    give = lax.dynamic_index_in_dim(part, 1 - core, 2, keepdims=False).astype(BF16)
    taken = lax.ppermute(give, "core", [(0, 1), (1, 0)])
    part = (keep + taken.astype(F32)).astype(BF16)
    part = lax.all_to_all(part, "x", 0, 0, tiled=True)
    part = jnp.sum(part.astype(F32), axis=0).astype(BF16)
    part = lax.all_to_all(part, "y", 0, 0, tiled=True)
    input_grad = jnp.sum(part.astype(F32), axis=0).astype(BF16)

    summed, input_grad = lax.optimization_barrier((summed, input_grad))
    summed = summed.astype(F32)
    square = jnp.sum(summed * summed)
    spread = jnp.broadcast_to(square, (NX * NY * NC, 128))
    square = jnp.sum(lax.all_to_all(spread, TENSOR, 0, 0, tiled=True)[:, :1])
    spread = jnp.broadcast_to(square, (N_SEQ, 8, 128))
    square = jnp.sum(lax.all_to_all(spread, "seq", 0, 0, tiled=True)[:, :1, :1])
    entries = width * 3 * DH * (NX * NY * NC)
    factor = jnp.minimum(1.0, CLIP_RMS * math.sqrt(entries) / jnp.sqrt(square + 1e-06))
    return (input_grad, (summed * factor).astype(BF16))


def solution(mesh):
    fine = Mesh(mesh.devices.reshape(N_SEQ, NX, NY, NC), ("seq",) + TENSOR)
    return jax.shard_map(
        body,
        mesh=fine,
        in_specs=(P("seq", None), P(None, None, TENSOR), P("seq", TENSOR), P(TENSOR), P()),
        out_specs=(P(TENSOR, "seq"), P("seq", None, TENSOR)),
        check_vma=False,
    )
```

```python
import math

import jax
import jax.numpy as jnp
from jax import lax
from jax.experimental import pallas as pl
from jax.experimental.pallas import tpu as pltpu
from jax.sharding import Mesh, PartitionSpec as P

DH = 96
TOK = 192
D = 6144
N_SEQ = 12
NX, NY, NC = 4, 8, 2
N_TENSOR = NX * NY * NC
OUT_ROWS = D // N_TENSOR
HALF = D // NC
PER_X = HALF // NX
PARTS = 3 * DH
K_BLOCK = 1024
S_BLOCK = 1536

DROP_LOGARITHM = 0.3
CLIP_RMS = 0.5
SCALE = DH ** (-0.5)
F32 = jnp.float32
BF16 = jnp.bfloat16
TENSOR = ("x", "y", "core")

NN = (((1,), (0,)), ((), ()))
NT = (((1,), (1,)), ((), ()))
TN = (((0,), (0,)), ((), ()))


def dot(a, b, dims):
    return lax.dot_general(a, b, dims, preferred_element_type=F32)


def split(a):
    high = a.astype(BF16)
    return high, (a - high.astype(F32)).astype(BF16)


def dot_wide_left(a, b, dims):
    high, low = split(a)
    return dot(high, b, dims) + dot(low, b, dims)


def dot_wide_right(a, b, dims):
    high, low = split(b)
    return dot(a, high, dims) + dot(a, low, dims)


def log_decay(rate, events, first, steps):
    seen = jnp.zeros(steps.shape, F32)
    for k in range(events.shape[0]):
        place = events[k] - first
        seen += jnp.where((steps >= place) & (place >= 0), 1.0, 0.0)
    return -(rate * (steps + 1).astype(F32) + DROP_LOGARITHM * seen)


def tail_and_head(rate, events, first):
    steps = lax.broadcasted_iota(jnp.int32, (TOK, 1), 0)
    cumul = log_decay(rate, events, first, steps)
    total = log_decay(rate, events, first, jnp.full((1, 1), TOK - 1, jnp.int32))
    return jnp.exp(total - cumul), jnp.exp(cumul)


def project_kernel(rate_ref, events_ref, x_ref, w_ref, o_ref, qkv_ref, send_ref, acc):
    step = pl.program_id(0)
    term = dot(x_ref[...], w_ref[...], NT)

    @pl.when(step == 0)
    def _():
        acc[...] = term

    @pl.when(step > 0)
    def _():
        acc[...] += term

    @pl.when(step == pl.num_programs(0) - 1)
    def _():
        me = lax.axis_index("seq")
        first = me * TOK
        rate = rate_ref[0]
        proj = acc[...]
        query = (proj[:, :DH] * SCALE).astype(BF16)
        keys = proj[:, DH : 2 * DH].astype(BF16)
        values = proj[:, 2 * DH :].astype(BF16)
        qkv_ref[0] = query
        qkv_ref[1] = keys
        qkv_ref[2] = values
        tail_w, head_w = tail_and_head(rate, events_ref, first)
        forward = dot_wide_left(values.astype(F32) * tail_w, keys, TN)
        reverse = dot_wide_left(query.astype(F32) * head_w, o_ref[...], TN)
        for d in range(N_SEQ):
            low = (jnp.minimum(me, d) + 1) * TOK
            high = jnp.maximum(me, d) * TOK
            count = jnp.float32(0.0)
            for k in range(events_ref.shape[0]):
                inside = (events_ref[k] >= low) & (events_ref[k] < high)
                count += jnp.where(inside, 1.0, 0.0)
            gap = jnp.maximum(high - low, 0).astype(F32)
            weight = jnp.exp(jnp.full((1, DH), -(rate * gap + DROP_LOGARITHM * count), F32))
            send_ref[d] = (jnp.where(d > me, forward, reverse) * weight).astype(BF16)


def local_kernel(rate_ref, events_ref, qkv_ref, o_ref, w_ref, grads_ref, half_ref):
    core = lax.axis_index("core")
    block = w_ref[...]
    for c in range(NC):
        mine = jnp.concatenate(
            [block[:, (y * NC + c) * OUT_ROWS : (y * NC + c + 1) * OUT_ROWS] for y in range(NY)],
            axis=1,
        )
        half_ref[lax.rem(core + c, NC)] = mine

    @pl.when(pl.program_id(0) == 0)
    def _():
        first = lax.axis_index("seq") * TOK
        rate = rate_ref[0]
        row = lax.broadcasted_iota(jnp.int32, (TOK, 1), 0)
        column = lax.broadcasted_iota(jnp.int32, (1, TOK), 1)
        later = row >= column
        gap = log_decay(rate, events_ref, first, row) - log_decay(rate, events_ref, first, column)
        weight = jnp.where(later, jnp.exp(jnp.where(later, gap, 0.0)), 0.0)
        query, keys, values, out = qkv_ref[0], qkv_ref[1], qkv_ref[2], o_ref[...]
        scores = dot(query, keys, NT) * weight
        dscores = dot(out, values, NT) * weight
        grads_ref[0] = dot_wide_left(dscores, keys, NN)
        grads_ref[1] = dot_wide_left(dscores, query, TN)
        grads_ref[2] = dot_wide_left(scores, out, TN)


def weight_kernel(rate_ref, events_ref, got_ref, local_ref, qkv_ref, o_ref, x_ref, grads_ref, terms_ref):
    @pl.when(pl.program_id(0) == 0)
    def _():
        me = lax.axis_index("seq")
        tail_w, head_w = tail_and_head(rate_ref[0], events_ref, me * TOK)
        prefix = jnp.zeros((DH, DH), F32)
        suffix = jnp.zeros((DH, DH), F32)
        for j in range(N_SEQ):
            state = got_ref[j].astype(F32)
            prefix += jnp.where(j < me, state, 0.0)
            suffix += jnp.where(j > me, state, 0.0)
        dquery = local_ref[0] + head_w * dot_wide_right(o_ref[...], prefix, NN)
        dkey = local_ref[1] + tail_w * dot_wide_right(qkv_ref[2], suffix, NT)
        dvalue = local_ref[2] + tail_w * dot_wide_right(qkv_ref[1], suffix, NN)
        grads_ref[...] = jnp.concatenate([dquery * SCALE, dkey, dvalue], axis=1).astype(BF16)

    terms_ref[...] = dot(grads_ref[...], x_ref[...], TN).astype(BF16)


def give_kernel(grads_ref, w_ref, give_ref):
    give_ref[...] = dot(grads_ref[...], w_ref[...], NN).astype(BF16)


def keep_kernel(grads_ref, w_ref, taken_ref, sum_ref):
    sum_ref[...] = (dot(grads_ref[...], w_ref[...], NN) + taken_ref[...].astype(F32)).astype(BF16)


def add_x_kernel(part_ref, out_ref):
    total = part_ref[0].astype(F32)
    for j in range(1, NX):
        total += part_ref[j].astype(F32)
    total = total.T.astype(BF16)
    for y in range(NY):
        out_ref[y] = total[y * OUT_ROWS : (y + 1) * OUT_ROWS]


def add_y_kernel(part_ref, out_ref):
    total = part_ref[0].astype(F32)
    for j in range(1, NY):
        total += part_ref[j].astype(F32)
    out_ref[...] = total.astype(BF16)


SMEM = pl.BlockSpec(memory_space=pltpu.SMEM)


def whole(*shape):
    return pl.BlockSpec(shape, lambda i: (0,) * len(shape))


def shape_of(shape, dtype=BF16):
    return jax.ShapeDtypeStruct(shape, dtype)


def call(kernel, grid, in_specs, out_specs, out_shape, cost, scratch=()):
    flops, moved = cost
    return pl.pallas_call(
        kernel,
        grid=(grid,),
        in_specs=in_specs,
        out_specs=out_specs,
        out_shape=out_shape,
        scratch_shapes=list(scratch),
        compiler_params=pltpu.CompilerParams(
            dimension_semantics=("arbitrary",), vmem_limit_bytes=24 << 20
        ),
        cost_estimate=pl.CostEstimate(flops=flops, bytes_accessed=moved, transcendentals=0),
    )


def project(rate, events, x, w, o):
    return call(
        project_kernel,
        D // K_BLOCK,
        [
            SMEM,
            SMEM,
            pl.BlockSpec((TOK, K_BLOCK), lambda i: (0, i)),
            pl.BlockSpec((PARTS, K_BLOCK), lambda i: (0, i)),
            whole(TOK, DH),
        ],
        [whole(3, TOK, DH), whole(N_SEQ, DH, DH)],
        [shape_of((3, TOK, DH)), shape_of((N_SEQ, DH, DH))],
        (2 * TOK * D * PARTS, 2 * D * (TOK + PARTS)),
        [pltpu.VMEM((TOK, PARTS), F32)],
    )(rate, events, x, w, o)


def local_part(rate, events, qkv, o, w):
    return call(
        local_kernel,
        NX,
        [
            SMEM,
            SMEM,
            whole(3, TOK, DH),
            whole(TOK, DH),
            pl.BlockSpec((PARTS, D // NX), lambda i: (0, i)),
        ],
        [whole(3, TOK, DH), pl.BlockSpec((NC, PARTS, PER_X), lambda i: (0, 0, i))],
        [shape_of((3, TOK, DH), F32), shape_of((NC, PARTS, HALF))],
        (20 * TOK * TOK * DH, 4 * D * PARTS),
    )(rate, events, qkv, o, w)


def weight_terms(rate, events, got, local, qkv, o, x):
    return call(
        weight_kernel,
        D // S_BLOCK,
        [
            SMEM,
            SMEM,
            whole(N_SEQ, DH, DH),
            whole(3, TOK, DH),
            whole(3, TOK, DH),
            whole(TOK, DH),
            pl.BlockSpec((TOK, S_BLOCK), lambda i: (0, i)),
        ],
        [whole(TOK, PARTS), pl.BlockSpec((PARTS, S_BLOCK), lambda i: (0, i))],
        [shape_of((TOK, PARTS)), shape_of((PARTS, D))],
        (2 * TOK * D * PARTS, 2 * D * (TOK + PARTS)),
    )(rate, events, got, local, qkv, o, x)


def half_spec(which):
    return pl.BlockSpec((None, PARTS, PER_X), lambda i: (which, 0, i))


CHUNK = pl.BlockSpec((None, TOK, PER_X), lambda i: (i, 0, 0))


def give_part(grads, halves):
    return call(
        give_kernel,
        NX,
        [whole(TOK, PARTS), half_spec(1)],
        CHUNK,
        shape_of((NX, TOK, PER_X)),
        (TOK * D * PARTS, D * (TOK + PARTS)),
    )(grads, halves)


def keep_part(grads, halves, taken):
    return call(
        keep_kernel,
        NX,
        [whole(TOK, PARTS), half_spec(0), CHUNK],
        CHUNK,
        shape_of((NX, TOK, PER_X)),
        (TOK * D * PARTS, D * (2 * TOK + PARTS)),
    )(grads, halves, taken)


def add_x(parts):
    return call(
        add_x_kernel,
        1,
        [whole(NX, TOK, PER_X)],
        whole(NY, OUT_ROWS, TOK),
        shape_of((NY, OUT_ROWS, TOK)),
        (4 * TOK * PER_X, 10 * TOK * PER_X),
    )(parts)


def add_y(parts):
    return call(
        add_y_kernel,
        1,
        [whole(NY, OUT_ROWS, TOK)],
        whole(OUT_ROWS, TOK),
        shape_of((OUT_ROWS, TOK)),
        (TOK * PER_X, 2 * TOK * PER_X),
    )(parts)


def body(layer_inputs, projection_matrices, result_sensitivity, channel_fading_rate, loss_events):
    x, o, rate, events = layer_inputs, result_sensitivity, channel_fading_rate, loss_events
    w = projection_matrices.transpose(1, 2, 0).reshape(PARTS, D)
    qkv, send = project(rate, events, x, w, o)
    got = lax.all_to_all(send, "seq", 0, 0, tiled=True)
    local, halves = local_part(rate, events, qkv, o, w)
    grads, terms = weight_terms(rate, events, got, local, qkv, o, x)
    summed = lax.psum_scatter(terms, "seq", scatter_dimension=1, tiled=True)

    give = give_part(grads, halves)
    taken = lax.ppermute(give, "core", [(0, 1), (1, 0)])
    part = keep_part(grads, halves, taken)
    part = add_x(lax.all_to_all(part, "x", 0, 0, tiled=True))
    input_grad = add_y(lax.all_to_all(part, "y", 0, 0, tiled=True))

    summed, input_grad = lax.optimization_barrier((summed, input_grad))
    summed = summed.astype(F32)
    square = jnp.sum(summed * summed)
    spread = jnp.broadcast_to(square, (N_TENSOR, 128))
    square = jnp.sum(lax.all_to_all(spread, TENSOR, 0, 0, tiled=True)[:, :1])
    spread = jnp.broadcast_to(square, (N_SEQ, 8, 128))
    square = jnp.sum(lax.all_to_all(spread, "seq", 0, 0, tiled=True)[:, :1, :1])
    factor = jnp.minimum(1.0, CLIP_RMS * math.sqrt(D * PARTS * N_TENSOR) / jnp.sqrt(square + 1e-06))
    weight_grad = (summed * factor).astype(BF16)
    return (input_grad, weight_grad.reshape(3, DH, D // N_SEQ).transpose(2, 0, 1))


def solution(mesh):
    fine = Mesh(mesh.devices.reshape(N_SEQ, NX, NY, NC), ("seq",) + TENSOR)
    return jax.shard_map(
        body,
        mesh=fine,
        in_specs=(P("seq", None), P(None, None, TENSOR), P("seq", TENSOR), P(TENSOR), P()),
        out_specs=(P(TENSOR, "seq"), P("seq", None, TENSOR)),
        check_vma=False,
    )
```

```python
import math

import jax
import jax.numpy as jnp
from jax import lax
from jax.experimental import pallas as pl
from jax.experimental.pallas import tpu as pltpu
from jax.sharding import Mesh, PartitionSpec as P

DH = 96
TOK = 192
D = 6144
N_SEQ = 12
NX, NY, NC = 4, 8, 2
N_TENSOR = NX * NY * NC
OUT_ROWS = D // N_TENSOR
HALF = D // NC
PER_X = HALF // NX
PARTS = 3 * DH
K_BLOCK = 1024
S_BLOCK = 1536
VMEM_LIMIT = 60 << 20

DROP_LOGARITHM = 0.3
CLIP_RMS = 0.5
SCALE = DH ** (-0.5)
F32 = jnp.float32
BF16 = jnp.bfloat16
TENSOR = ("x", "y", "core")

NN = (((1,), (0,)), ((), ()))
NT = (((1,), (1,)), ((), ()))
TN = (((0,), (0,)), ((), ()))


def dot(a, b, dims):
    return lax.dot_general(a, b, dims, preferred_element_type=F32)


def split(a):
    high = a.astype(BF16)
    return high, (a - high.astype(F32)).astype(BF16)


def dot_wide_left(a, b, dims):
    high, low = split(a)
    return dot(high, b, dims) + dot(low, b, dims)


def dot_wide_right(a, b, dims):
    high, low = split(b)
    return dot(a, high, dims) + dot(a, low, dims)


def log_decay(rate, events, first, steps):
    seen = jnp.zeros(steps.shape, F32)
    for k in range(events.shape[0]):
        place = events[k] - first
        seen += jnp.where((steps >= place) & (place >= 0), 1.0, 0.0)
    return -(rate * (steps + 1).astype(F32) + DROP_LOGARITHM * seen)


def tail_and_head(rate, events, first):
    steps = lax.broadcasted_iota(jnp.int32, (TOK, 1), 0)
    cumul = log_decay(rate, events, first, steps)
    total = log_decay(rate, events, first, jnp.full((1, 1), TOK - 1, jnp.int32))
    return jnp.exp(total - cumul), jnp.exp(cumul)


def project_kernel(rate_ref, events_ref, x_ref, w_ref, o_ref, qkv_ref, send_ref, acc):
    step = pl.program_id(0)
    term = dot(x_ref[...], w_ref[...], NT)

    @pl.when(step == 0)
    def _():
        acc[...] = term

    @pl.when(step > 0)
    def _():
        acc[...] += term

    @pl.when(step == pl.num_programs(0) - 1)
    def _():
        me = lax.axis_index("seq")
        first = me * TOK
        rate = rate_ref[0]
        proj = acc[...]
        query = (proj[:, :DH] * SCALE).astype(BF16)
        keys = proj[:, DH : 2 * DH].astype(BF16)
        values = proj[:, 2 * DH :].astype(BF16)
        qkv_ref[0] = query
        qkv_ref[1] = keys
        qkv_ref[2] = values
        tail_w, head_w = tail_and_head(rate, events_ref, first)
        forward = dot_wide_left(values.astype(F32) * tail_w, keys, TN)
        reverse = dot_wide_left(query.astype(F32) * head_w, o_ref[...], TN)
        for d in range(N_SEQ):
            low = (jnp.minimum(me, d) + 1) * TOK
            high = jnp.maximum(me, d) * TOK
            count = jnp.float32(0.0)
            for k in range(events_ref.shape[0]):
                inside = (events_ref[k] >= low) & (events_ref[k] < high)
                count += jnp.where(inside, 1.0, 0.0)
            gap = jnp.maximum(high - low, 0).astype(F32)
            weight = jnp.exp(jnp.full((1, DH), -(rate * gap + DROP_LOGARITHM * count), F32))
            send_ref[d] = (jnp.where(d > me, forward, reverse) * weight).astype(BF16)


def local_kernel(rate_ref, events_ref, qkv_ref, o_ref, w_ref, grads_ref, half_ref):
    core = lax.axis_index("core")
    block = w_ref[...]
    for c in range(NC):
        mine = jnp.concatenate(
            [block[:, (y * NC + c) * OUT_ROWS : (y * NC + c + 1) * OUT_ROWS] for y in range(NY)],
            axis=1,
        )
        half_ref[lax.rem(core + c, NC)] = mine

    @pl.when(pl.program_id(0) == 0)
    def _():
        first = lax.axis_index("seq") * TOK
        rate = rate_ref[0]
        row = lax.broadcasted_iota(jnp.int32, (TOK, 1), 0)
        column = lax.broadcasted_iota(jnp.int32, (1, TOK), 1)
        later = row >= column
        gap = log_decay(rate, events_ref, first, row) - log_decay(rate, events_ref, first, column)
        weight = jnp.where(later, jnp.exp(jnp.where(later, gap, 0.0)), 0.0)
        query, keys, values, out = qkv_ref[0], qkv_ref[1], qkv_ref[2], o_ref[...]
        scores = dot(query, keys, NT) * weight
        dscores = dot(out, values, NT) * weight
        grads_ref[0] = dot_wide_left(dscores, keys, NN)
        grads_ref[1] = dot_wide_left(dscores, query, TN)
        grads_ref[2] = dot_wide_left(scores, out, TN)


def weight_kernel(rate_ref, events_ref, got_ref, local_ref, qkv_ref, o_ref, x_ref, grads_ref, terms_ref):
    @pl.when(pl.program_id(0) == 0)
    def _():
        me = lax.axis_index("seq")
        tail_w, head_w = tail_and_head(rate_ref[0], events_ref, me * TOK)
        prefix = jnp.zeros((DH, DH), F32)
        suffix = jnp.zeros((DH, DH), F32)
        for j in range(N_SEQ):
            state = got_ref[j].astype(F32)
            prefix += jnp.where(j < me, state, 0.0)
            suffix += jnp.where(j > me, state, 0.0)
        dquery = local_ref[0] + head_w * dot_wide_right(o_ref[...], prefix, NN)
        dkey = local_ref[1] + tail_w * dot_wide_right(qkv_ref[2], suffix, NT)
        dvalue = local_ref[2] + tail_w * dot_wide_right(qkv_ref[1], suffix, NN)
        grads_ref[...] = jnp.concatenate([dquery * SCALE, dkey, dvalue], axis=1).astype(BF16)

    terms_ref[...] = dot(grads_ref[...], x_ref[...], TN).astype(BF16)


def give_kernel(grads_ref, w_ref, give_ref):
    give_ref[...] = dot(grads_ref[...], w_ref[...], NN).astype(BF16)


def keep_kernel(grads_ref, w_ref, taken_ref, sum_ref):
    sum_ref[...] = (dot(grads_ref[...], w_ref[...], NN) + taken_ref[...].astype(F32)).astype(BF16)


def add_x_kernel(part_ref, out_ref):
    total = part_ref[0].astype(F32)
    for j in range(1, NX):
        total += part_ref[j].astype(F32)
    total = total.T.astype(BF16)
    for y in range(NY):
        out_ref[y] = total[y * OUT_ROWS : (y + 1) * OUT_ROWS]


def add_y_kernel(part_ref, out_ref):
    total = part_ref[0].astype(F32)
    for j in range(1, NY):
        total += part_ref[j].astype(F32)
    out_ref[...] = total.astype(BF16)


def square_kernel(summed_ref, out_ref):
    summed = summed_ref[...].astype(F32)
    total = jnp.sum(jnp.sum(summed * summed, axis=0, keepdims=True), axis=1, keepdims=True)
    out_ref[...] = jnp.broadcast_to(total, out_ref.shape)


def sum_kernel(parts_ref, out_ref):
    total = jnp.sum(parts_ref[...], axis=0, keepdims=True)
    out_ref[...] = jnp.broadcast_to(total[None], out_ref.shape)


def scale_kernel(parts_ref, summed_ref, out_ref):
    square = jnp.sum(parts_ref[...], axis=0)[:1, :1]
    limit = CLIP_RMS * math.sqrt(D * PARTS * N_TENSOR)
    factor = jnp.minimum(1.0, limit * lax.rsqrt(square + 1e-06))
    out_ref[...] = (summed_ref[...].astype(F32) * factor).astype(BF16)


SMEM = pl.BlockSpec(memory_space=pltpu.SMEM)


def whole(*shape):
    return pl.BlockSpec(shape, lambda i: (0,) * len(shape))


def shape_of(shape, dtype=BF16):
    return jax.ShapeDtypeStruct(shape, dtype)


def call(kernel, grid, in_specs, out_specs, out_shape, cost, scratch=()):
    flops, moved = cost
    return pl.pallas_call(
        kernel,
        grid=(grid,),
        in_specs=in_specs,
        out_specs=out_specs,
        out_shape=out_shape,
        scratch_shapes=list(scratch),
        compiler_params=pltpu.CompilerParams(
            dimension_semantics=("arbitrary",), vmem_limit_bytes=VMEM_LIMIT
        ),
        cost_estimate=pl.CostEstimate(flops=flops, bytes_accessed=moved, transcendentals=0),
    )


def project(rate, events, x, w, o):
    return call(
        project_kernel,
        D // K_BLOCK,
        [
            SMEM,
            SMEM,
            pl.BlockSpec((TOK, K_BLOCK), lambda i: (0, i)),
            pl.BlockSpec((PARTS, K_BLOCK), lambda i: (0, i)),
            whole(TOK, DH),
        ],
        [whole(3, TOK, DH), whole(N_SEQ, DH, DH)],
        [shape_of((3, TOK, DH)), shape_of((N_SEQ, DH, DH))],
        (2 * TOK * D * PARTS, 2 * D * (TOK + PARTS)),
        [pltpu.VMEM((TOK, PARTS), F32)],
    )(rate, events, x, w, o)


def local_part(rate, events, qkv, o, w):
    return call(
        local_kernel,
        NX,
        [
            SMEM,
            SMEM,
            whole(3, TOK, DH),
            whole(TOK, DH),
            pl.BlockSpec((PARTS, D // NX), lambda i: (0, i)),
        ],
        [whole(3, TOK, DH), pl.BlockSpec((NC, PARTS, PER_X), lambda i: (0, 0, i))],
        [shape_of((3, TOK, DH), F32), shape_of((NC, PARTS, HALF))],
        (20 * TOK * TOK * DH, 4 * D * PARTS),
    )(rate, events, qkv, o, w)


def weight_terms(rate, events, got, local, qkv, o, x):
    return call(
        weight_kernel,
        D // S_BLOCK,
        [
            SMEM,
            SMEM,
            whole(N_SEQ, DH, DH),
            whole(3, TOK, DH),
            whole(3, TOK, DH),
            whole(TOK, DH),
            pl.BlockSpec((TOK, S_BLOCK), lambda i: (0, i)),
        ],
        [whole(TOK, PARTS), pl.BlockSpec((PARTS, S_BLOCK), lambda i: (0, i))],
        [shape_of((TOK, PARTS)), shape_of((PARTS, D))],
        (2 * TOK * D * PARTS, 2 * D * (TOK + PARTS)),
    )(rate, events, got, local, qkv, o, x)


def half_spec(which):
    return pl.BlockSpec((None, PARTS, PER_X), lambda i: (which, 0, i))


CHUNK = pl.BlockSpec((None, TOK, PER_X), lambda i: (i, 0, 0))


def give_part(grads, halves):
    return call(
        give_kernel,
        NX,
        [whole(TOK, PARTS), half_spec(1)],
        CHUNK,
        shape_of((NX, TOK, PER_X)),
        (TOK * D * PARTS, D * (TOK + PARTS)),
    )(grads, halves)


def keep_part(grads, halves, taken):
    return call(
        keep_kernel,
        NX,
        [whole(TOK, PARTS), half_spec(0), CHUNK],
        CHUNK,
        shape_of((NX, TOK, PER_X)),
        (TOK * D * PARTS, D * (2 * TOK + PARTS)),
    )(grads, halves, taken)


def add_x(parts):
    return call(
        add_x_kernel,
        1,
        [whole(NX, TOK, PER_X)],
        whole(NY, OUT_ROWS, TOK),
        shape_of((NY, OUT_ROWS, TOK)),
        (4 * TOK * PER_X, 10 * TOK * PER_X),
    )(parts)


def add_y(parts):
    return call(
        add_y_kernel,
        1,
        [whole(NY, OUT_ROWS, TOK)],
        whole(OUT_ROWS, TOK),
        shape_of((OUT_ROWS, TOK)),
        (TOK * PER_X, 2 * TOK * PER_X),
    )(parts)


def square_of(summed):
    return call(
        square_kernel,
        1,
        [whole(*summed.shape)],
        whole(N_TENSOR, 128),
        shape_of((N_TENSOR, 128), F32),
        (2 * summed.size, 2 * summed.size),
    )(summed)


def sum_of(parts):
    return call(
        sum_kernel,
        1,
        [whole(N_TENSOR, 128)],
        whole(N_SEQ, 8, 128),
        shape_of((N_SEQ, 8, 128), F32),
        (N_TENSOR * 128, 4 * N_TENSOR * 128),
    )(parts)


def scaled(parts, summed):
    return call(
        scale_kernel,
        1,
        [whole(N_SEQ, 8, 128), whole(*summed.shape)],
        whole(*summed.shape),
        shape_of(summed.shape),
        (2 * summed.size, 4 * summed.size),
    )(parts, summed)


def body(layer_inputs, projection_matrices, result_sensitivity, channel_fading_rate, loss_events):
    x, o, rate, events = layer_inputs, result_sensitivity, channel_fading_rate, loss_events
    w = projection_matrices.transpose(1, 2, 0).reshape(PARTS, D)
    qkv, send = project(rate, events, x, w, o)
    got = lax.all_to_all(send, "seq", 0, 0, tiled=True)
    local, halves = local_part(rate, events, qkv, o, w)
    grads, terms = weight_terms(rate, events, got, local, qkv, o, x)
    summed = lax.psum_scatter(terms, "seq", scatter_dimension=1, tiled=True)

    give = give_part(grads, halves)
    taken = lax.ppermute(give, "core", [(0, 1), (1, 0)])
    part = keep_part(grads, halves, taken)
    part = add_x(lax.all_to_all(part, "x", 0, 0, tiled=True))
    input_grad = add_y(lax.all_to_all(part, "y", 0, 0, tiled=True))

    summed, input_grad = lax.optimization_barrier((summed, input_grad))
    square = lax.all_to_all(square_of(summed), TENSOR, 0, 0, tiled=True)
    square = lax.all_to_all(sum_of(square), "seq", 0, 0, tiled=True)
    weight_grad = scaled(square, summed)
    return (input_grad, weight_grad.reshape(3, DH, D // N_SEQ).transpose(2, 0, 1))


def solution(mesh):
    fine = Mesh(mesh.devices.reshape(N_SEQ, NX, NY, NC), ("seq",) + TENSOR)
    return jax.shard_map(
        body,
        mesh=fine,
        in_specs=(P("seq", None), P(None, None, TENSOR), P("seq", TENSOR), P(TENSOR), P()),
        out_specs=(P(TENSOR, "seq"), P("seq", None, TENSOR)),
        check_vma=False,
    )
```

```python
import math

import jax
import jax.numpy as jnp
from jax import lax
from jax.experimental import pallas as pl
from jax.experimental.pallas import tpu as pltpu
from jax.sharding import Mesh, PartitionSpec as P

DH = 96
TOK = 192
D = 6144
N_SEQ = 12
NX, NY, NC = 4, 8, 2
N_TENSOR = NX * NY * NC
OUT_ROWS = D // N_TENSOR
HALF = D // NC
PER_X = HALF // NX
PARTS = 3 * DH
K_BLOCK = 1536
S_BLOCK = 1536
PACK_ROWS = 72
PACK_REST = 32
BIG = 60 << 20
MIDDLE = 50 << 20
SMALL = 8 << 20

DROP_LOGARITHM = 0.3
CLIP_RMS = 0.5
SCALE = DH ** (-0.5)
F32 = jnp.float32
BF16 = jnp.bfloat16
TENSOR = ("x", "y", "core")

NN = (((1,), (0,)), ((), ()))
NT = (((1,), (1,)), ((), ()))
TN = (((0,), (0,)), ((), ()))
TT = (((0,), (1,)), ((), ()))


def dot(a, b, dims):
    return lax.dot_general(a, b, dims, preferred_element_type=F32)


def split(a):
    high = a.astype(BF16)
    return high, (a - high.astype(F32)).astype(BF16)


def dot_wide_left(a, b, dims):
    high, low = split(a)
    return dot(high, b, dims) + dot(low, b, dims)


def dot_wide_right(a, b, dims):
    high, low = split(b)
    return dot(a, high, dims) + dot(a, low, dims)


def log_decay(rate, events, first, steps):
    seen = jnp.zeros(steps.shape, F32)
    for k in range(events.shape[0]):
        place = events[k] - first
        seen += jnp.where((steps >= place) & (place >= 0), 1.0, 0.0)
    return -(rate * (steps + 1).astype(F32) + DROP_LOGARITHM * seen)


def tail_and_head(rate, events, first):
    steps = lax.broadcasted_iota(jnp.int32, (1, TOK), 1)
    cumul = log_decay(rate, events, first, steps)
    total = log_decay(rate, events, first, jnp.full((1, 1), TOK - 1, jnp.int32))
    return jnp.exp(total - cumul), jnp.exp(cumul)


def pack(state):
    rest = [state[PACK_ROWS:, k * PACK_REST : (k + 1) * PACK_REST] for k in range(DH // PACK_REST)]
    return jnp.concatenate([state[:PACK_ROWS], jnp.concatenate(rest, axis=0)], axis=1)


def unpack(packed):
    rows = DH - PACK_ROWS
    rest = [packed[k * rows : (k + 1) * rows, DH:] for k in range(DH // PACK_REST)]
    return jnp.concatenate([packed[:, :DH], jnp.concatenate(rest, axis=1)], axis=0)


def columns(k, size):
    return pl.ds(k * size, size)


def fetch(pairs, sems):
    copies = [pltpu.make_async_copy(a, b, sems.at[k]) for k, (a, b) in enumerate(pairs)]
    for copy in copies:
        copy.start()
    return copies


def wait(copies):
    for copy in copies:
        copy.wait()


def project_kernel(
    rate_ref, events_ref, x_ref, w_ref, o_ref, qkv_ref, send_ref,
    x_buf, w_buf, o_buf, acc, sems, o_sem,
):
    copies = []
    for k in range(D // K_BLOCK):
        at = columns(k, K_BLOCK)
        pair = (
            pltpu.make_async_copy(x_ref.at[:, at], x_buf.at[:, at], sems.at[0, k]),
            pltpu.make_async_copy(w_ref.at[:, at], w_buf.at[:, at], sems.at[1, k]),
        )
        for copy in pair:
            copy.start()
        copies.append(pair)
    o_copy = fetch([(o_ref, o_buf)], o_sem)
    for k, pair in enumerate(copies):
        wait(pair)
        at = columns(k, K_BLOCK)
        term = dot(w_buf[:, at], x_buf[:, at], NT)
        if k == 0:
            acc[...] = term
        else:
            acc[...] += term

    me = lax.axis_index("seq")
    rate = rate_ref[0]
    query = (acc[:DH] * SCALE).astype(BF16)
    keys = acc[DH : 2 * DH].astype(BF16)
    values = acc[2 * DH :].astype(BF16)
    qkv_ref[0] = query
    qkv_ref[1] = keys
    qkv_ref[2] = values
    tail_w, head_w = tail_and_head(rate, events_ref, me * TOK)
    forward = pack(dot_wide_left(values.astype(F32) * tail_w, keys, NT))
    wait(o_copy)
    reverse = pack(dot_wide_left(query.astype(F32) * head_w, o_buf[...], NN))
    for d in range(N_SEQ):
        low = (jnp.minimum(me, d) + 1) * TOK
        high = jnp.maximum(me, d) * TOK
        count = jnp.float32(0.0)
        for k in range(events_ref.shape[0]):
            inside = (events_ref[k] >= low) & (events_ref[k] < high)
            count += jnp.where(inside, 1.0, 0.0)
        gap = jnp.maximum(high - low, 0).astype(F32)
        weight = jnp.exp(jnp.full((1, 128), -(rate * gap + DROP_LOGARITHM * count), F32))
        send_ref[d] = (jnp.where(d > me, forward, reverse) * weight).astype(BF16)


def local_kernel(rate_ref, events_ref, qkv_ref, o_ref, w_ref, grads_ref, half_ref):
    core = lax.axis_index("core")
    block = w_ref[...]
    for c in range(NC):
        mine = jnp.concatenate(
            [block[:, (y * NC + c) * OUT_ROWS : (y * NC + c + 1) * OUT_ROWS] for y in range(NY)],
            axis=1,
        )
        half_ref[lax.rem(core + c, NC)] = mine

    @pl.when(pl.program_id(0) == 0)
    def _():
        first = lax.axis_index("seq") * TOK
        rate = rate_ref[0]
        row = lax.broadcasted_iota(jnp.int32, (TOK, 1), 0)
        column = lax.broadcasted_iota(jnp.int32, (1, TOK), 1)
        later = row >= column
        gap = log_decay(rate, events_ref, first, row) - log_decay(rate, events_ref, first, column)
        weight = jnp.where(later, jnp.exp(jnp.where(later, gap, 0.0)), 0.0)
        query, keys, values, out = qkv_ref[0], qkv_ref[1], qkv_ref[2], o_ref[...]
        scores = dot(query, keys, TN) * weight
        dscores = dot(out, values, NN) * weight
        grads_ref[:DH] = dot_wide_right(keys, dscores, NT)
        grads_ref[DH : 2 * DH] = dot_wide_right(query, dscores, NN)
        grads_ref[2 * DH :] = dot_wide_right(out, scores, TN)


def weight_kernel(
    rate_ref, events_ref, got_ref, local_ref, qkv_ref, o_ref, x_ref, grads_ref, terms_ref,
    terms_buf, sems,
):
    me = lax.axis_index("seq")
    tail_w, head_w = tail_and_head(rate_ref[0], events_ref, me * TOK)
    prefix = jnp.zeros((PACK_ROWS, 128), F32)
    suffix = jnp.zeros((PACK_ROWS, 128), F32)
    for j in range(N_SEQ):
        state = got_ref[j].astype(F32)
        prefix += jnp.where(j < me, state, 0.0)
        suffix += jnp.where(j > me, state, 0.0)
    prefix, suffix = unpack(prefix), unpack(suffix)
    dquery = local_ref[:DH] + head_w * dot_wide_left(prefix, o_ref[...], TT)
    dkey = local_ref[DH : 2 * DH] + tail_w * dot_wide_left(suffix, qkv_ref[2], NN)
    dvalue = local_ref[2 * DH :] + tail_w * dot_wide_left(suffix, qkv_ref[1], TN)
    grads_ref[:DH] = (dquery * SCALE).astype(BF16)
    grads_ref[DH : 2 * DH] = dkey.astype(BF16)
    grads_ref[2 * DH :] = dvalue.astype(BF16)

    grads = grads_ref[...]
    sent = []
    for k in range(D // S_BLOCK):
        at = columns(k, S_BLOCK)
        terms_buf[:, at] = dot(grads, x_ref[:, at], NN).astype(BF16)
        copy = pltpu.make_async_copy(terms_buf.at[:, at], terms_ref.at[:, at], sems.at[k])
        copy.start()
        sent.append(copy)
    wait(sent)


def half_copies(w_ref, w_buf, sems, which):
    chunks = [columns(k, PER_X) for k in range(NX)]
    return fetch([(w_ref.at[which, :, at], w_buf.at[:, at]) for at in chunks], sems)


def give_kernel(grads_ref, w_ref, give_ref, w_buf, sems):
    grads = grads_ref[...]
    for k, copy in enumerate(half_copies(w_ref, w_buf, sems, 1)):
        wait([copy])
        give_ref[k] = dot(grads, w_buf[:, columns(k, PER_X)], TN).astype(BF16)


def keep_kernel(grads_ref, w_ref, taken_ref, sum_ref, w_buf, sems):
    grads = grads_ref[...]
    for k, copy in enumerate(half_copies(w_ref, w_buf, sems, 0)):
        wait([copy])
        mine = dot(grads, w_buf[:, columns(k, PER_X)], TN)
        sum_ref[k] = (mine + taken_ref[k].astype(F32)).astype(BF16)


def add_x_kernel(part_ref, out_ref):
    total = part_ref[0].astype(F32)
    for j in range(1, NX):
        total += part_ref[j].astype(F32)
    total = total.T.astype(BF16)
    for y in range(NY):
        out_ref[y] = total[y * OUT_ROWS : (y + 1) * OUT_ROWS]


def add_y_kernel(part_ref, out_ref):
    total = part_ref[0].astype(F32)
    for j in range(1, NY):
        total += part_ref[j].astype(F32)
    out_ref[...] = total.astype(BF16)


def square_kernel(summed_ref, out_ref, held_ref):
    held_ref[...] = summed_ref[...]
    summed = summed_ref[...].astype(F32)
    total = jnp.sum(jnp.sum(summed * summed, axis=0, keepdims=True), axis=1, keepdims=True)
    out_ref[...] = jnp.broadcast_to(total, out_ref.shape)


def sum_kernel(parts_ref, out_ref):
    total = jnp.sum(parts_ref[...], axis=0, keepdims=True)
    for j in range(N_SEQ):
        out_ref[j] = total


def scale_kernel(parts_ref, summed_ref, out_ref):
    square = parts_ref[0]
    for j in range(1, N_SEQ):
        square += parts_ref[j]
    square = square[:, :1]
    limit = CLIP_RMS * math.sqrt(D * PARTS * N_TENSOR)
    factor = jnp.minimum(1.0, limit * lax.rsqrt(square + 1e-06))
    out_ref[...] = (summed_ref[...].astype(F32) * factor).astype(BF16)


SMEM = pl.BlockSpec(memory_space=pltpu.SMEM)
VMEM = pl.BlockSpec(memory_space=pltpu.VMEM)
HBM = pl.BlockSpec(memory_space=pltpu.HBM)
DMA = pltpu.SemaphoreType.DMA


def shape_of(shape, dtype=BF16):
    return jax.ShapeDtypeStruct(shape, dtype)


def call(kernel, in_specs, out_specs, out_shape, cost, scratch=(), limit=BIG, **grid):
    flops, moved = cost
    return pl.pallas_call(
        kernel,
        in_specs=in_specs,
        out_specs=out_specs,
        out_shape=out_shape,
        scratch_shapes=list(scratch),
        compiler_params=pltpu.CompilerParams(vmem_limit_bytes=limit),
        cost_estimate=pl.CostEstimate(flops=flops, bytes_accessed=moved, transcendentals=0),
        **grid,
    )


def project(rate, events, x, w, o):
    return call(
        project_kernel,
        [SMEM, SMEM, HBM, HBM, HBM],
        [VMEM, VMEM],
        [shape_of((3, DH, TOK)), shape_of((N_SEQ, PACK_ROWS, 128))],
        (2 * TOK * D * PARTS, 2 * D * (TOK + PARTS)),
        [
            pltpu.VMEM((TOK, D), BF16),
            pltpu.VMEM((PARTS, D), BF16),
            pltpu.VMEM((TOK, DH), BF16),
            pltpu.VMEM((PARTS, TOK), F32),
            DMA((2, D // K_BLOCK)),
            DMA((1,)),
        ],
    )(rate, events, x, w, o)


def local_part(rate, events, qkv, o, w):
    def whole(*shape):
        return pl.BlockSpec(shape, lambda i: (0,) * len(shape))

    return call(
        local_kernel,
        [
            SMEM,
            SMEM,
            whole(3, DH, TOK),
            whole(TOK, DH),
            pl.BlockSpec((PARTS, D // NX), lambda i: (0, i)),
        ],
        [whole(PARTS, TOK), pl.BlockSpec((NC, PARTS, PER_X), lambda i: (0, 0, i))],
        [shape_of((PARTS, TOK), F32), shape_of((NC, PARTS, HALF))],
        (20 * TOK * TOK * DH, 4 * D * PARTS),
        grid=(NX,),
    )(rate, events, qkv, o, w)


def weight_terms(rate, events, got, local, qkv, o, x):
    return call(
        weight_kernel,
        [SMEM, SMEM, VMEM, VMEM, VMEM, VMEM, VMEM],
        [VMEM, HBM],
        [shape_of((PARTS, TOK)), shape_of((PARTS, D))],
        (2 * TOK * D * PARTS, 2 * D * (TOK + PARTS)),
        [
            pltpu.VMEM((PARTS, D), BF16),
            DMA((D // S_BLOCK,)),
        ],
        limit=MIDDLE,
    )(rate, events, got, local, qkv, o, x)


def give_part(grads, halves):
    return call(
        give_kernel,
        [VMEM, HBM],
        VMEM,
        shape_of((NX, TOK, PER_X)),
        (TOK * D * PARTS, D * (TOK + PARTS)),
        [pltpu.VMEM((PARTS, HALF), BF16), DMA((NX,))],
        limit=MIDDLE,
    )(grads, halves)


def keep_part(grads, halves, taken):
    return call(
        keep_kernel,
        [VMEM, HBM, VMEM],
        VMEM,
        shape_of((NX, TOK, PER_X)),
        (TOK * D * PARTS, D * (2 * TOK + PARTS)),
        [pltpu.VMEM((PARTS, HALF), BF16), DMA((NX,))],
        limit=MIDDLE,
    )(grads, halves, taken)


def add_x(parts):
    shape = (NY, OUT_ROWS, TOK)
    return call(
        add_x_kernel, [VMEM], VMEM, shape_of(shape), (4 * parts.size, 4 * parts.size), limit=SMALL
    )(parts)


def add_y(parts):
    shape = (OUT_ROWS, TOK)
    return call(
        add_y_kernel, [VMEM], VMEM, shape_of(shape), (parts.size, 2 * parts.size), limit=SMALL
    )(parts)


def square_of(summed):
    return call(
        square_kernel,
        [VMEM],
        [VMEM, VMEM],
        [shape_of((N_TENSOR, 128), F32), shape_of(summed.shape)],
        (2 * summed.size, 2 * summed.size),
        limit=SMALL,
    )(summed)


def sum_of(parts):
    return call(
        sum_kernel, [VMEM], VMEM, shape_of((N_SEQ, 1, 128), F32), (parts.size, 4 * parts.size), limit=SMALL
    )(parts)


def scaled(parts, summed):
    return call(
        scale_kernel,
        [VMEM, VMEM],
        VMEM,
        shape_of(summed.shape),
        (2 * summed.size, 4 * summed.size),
        limit=SMALL,
    )(parts, summed)


def body(layer_inputs, projection_matrices, result_sensitivity, channel_fading_rate, loss_events):
    x, o, rate, events = layer_inputs, result_sensitivity, channel_fading_rate, loss_events
    w = projection_matrices.transpose(1, 2, 0).reshape(PARTS, D)
    qkv, send = project(rate, events, x, w, o)
    got = lax.all_to_all(send, "seq", 0, 0, tiled=True)
    local, halves = local_part(rate, events, qkv, o, w)
    grads, terms = weight_terms(rate, events, got, local, qkv, o, x)
    summed = lax.psum_scatter(terms, "seq", scatter_dimension=1, tiled=True)

    give = give_part(grads, halves)
    taken = lax.ppermute(give, "core", [(0, 1), (1, 0)])
    part = keep_part(grads, halves, taken)
    part = add_x(lax.all_to_all(part, "x", 0, 0, tiled=True))
    input_grad = add_y(lax.all_to_all(part, "y", 0, 0, tiled=True))

    summed, input_grad = lax.optimization_barrier((summed, input_grad))
    square, summed = square_of(summed)
    square = lax.all_to_all(square, TENSOR, 0, 0, tiled=True)
    square = lax.all_to_all(sum_of(square), "seq", 0, 0, tiled=True)
    weight_grad = scaled(square, summed)
    return (input_grad, weight_grad.reshape(3, DH, D // N_SEQ).transpose(2, 0, 1))


def solution(mesh):
    fine = Mesh(mesh.devices.reshape(N_SEQ, NX, NY, NC), ("seq",) + TENSOR)
    return jax.shard_map(
        body,
        mesh=fine,
        in_specs=(P("seq", None), P(None, None, TENSOR), P("seq", TENSOR), P(TENSOR), P()),
        out_specs=(P(TENSOR, "seq"), P("seq", None, TENSOR)),
        check_vma=False,
    )
```

```python
import math

import jax
import jax.numpy as jnp
from jax import lax
from jax.experimental import pallas as pl
from jax.experimental.pallas import tpu as pltpu
from jax.sharding import Mesh, PartitionSpec as P

DH = 96
TOK = 192
D = 6144
N_SEQ = 12
NX, NY, NC = 4, 8, 2
N_TENSOR = NX * NY * NC
OUT_ROWS = D // N_TENSOR
HALF = D // NC
PER_X = HALF // NX
PARTS = 3 * DH
K_BLOCK = 1536
S_BLOCK = 1536
PACK_ROWS = 72
PACK_REST = 32
BIG = 60 << 20
MIDDLE = 50 << 20
SMALL = 8 << 20

DROP_LOGARITHM = 0.3
CLIP_RMS = 0.5
SCALE = DH ** (-0.5)
F32 = jnp.float32
BF16 = jnp.bfloat16
TENSOR = ("x", "y", "core")

NN = (((1,), (0,)), ((), ()))
NT = (((1,), (1,)), ((), ()))
TN = (((0,), (0,)), ((), ()))
TT = (((0,), (1,)), ((), ()))


def dot(a, b, dims):
    return lax.dot_general(a, b, dims, preferred_element_type=F32)


def split(a):
    high = a.astype(BF16)
    return high, (a - high.astype(F32)).astype(BF16)


def dot_wide_left(a, b, dims):
    high, low = split(a)
    return dot(high, b, dims) + dot(low, b, dims)


def dot_wide_right(a, b, dims):
    high, low = split(b)
    return dot(a, high, dims) + dot(a, low, dims)


def log_decay(rate, events, first, steps):
    seen = jnp.zeros(steps.shape, F32)
    for k in range(events.shape[0]):
        place = events[k] - first
        seen += jnp.where((steps >= place) & (place >= 0), 1.0, 0.0)
    return -(rate * (steps + 1).astype(F32) + DROP_LOGARITHM * seen)


def tail_and_head(rate, events, first):
    steps = lax.broadcasted_iota(jnp.int32, (1, TOK), 1)
    cumul = log_decay(rate, events, first, steps)
    total = log_decay(rate, events, first, jnp.full((1, 1), TOK - 1, jnp.int32))
    return jnp.exp(total - cumul), jnp.exp(cumul)


def pack(state):
    rest = [state[PACK_ROWS:, k * PACK_REST : (k + 1) * PACK_REST] for k in range(DH // PACK_REST)]
    return jnp.concatenate([state[:PACK_ROWS], jnp.concatenate(rest, axis=0)], axis=1)


def unpack(packed):
    rows = DH - PACK_ROWS
    rest = [packed[k * rows : (k + 1) * rows, DH:] for k in range(DH // PACK_REST)]
    return jnp.concatenate([packed[:, :DH], jnp.concatenate(rest, axis=1)], axis=0)


def columns(k, size):
    return pl.ds(k * size, size)


def fetch(pairs, sems):
    copies = [pltpu.make_async_copy(a, b, sems.at[k]) for k, (a, b) in enumerate(pairs)]
    for copy in copies:
        copy.start()
    return copies


def wait(copies):
    for copy in copies:
        copy.wait()


def project_kernel(
    rate_ref, events_ref, x_ref, w_ref, o_ref, qkv_ref, send_ref,
    x_buf, w_buf, o_buf, acc, sems, o_sem,
):
    copies = []
    for k in range(D // K_BLOCK):
        at = columns(k, K_BLOCK)
        pair = (
            pltpu.make_async_copy(x_ref.at[:, at], x_buf.at[:, at], sems.at[0, k]),
            pltpu.make_async_copy(w_ref.at[:, at], w_buf.at[:, at], sems.at[1, k]),
        )
        for copy in pair:
            copy.start()
        copies.append(pair)
    o_copy = fetch([(o_ref, o_buf)], o_sem)
    for k, pair in enumerate(copies):
        wait(pair)
        at = columns(k, K_BLOCK)
        term = dot(w_buf[:, at], x_buf[:, at], NT)
        if k == 0:
            acc[...] = term
        else:
            acc[...] += term

    me = lax.axis_index("seq")
    rate = rate_ref[0]
    query = (acc[:DH] * SCALE).astype(BF16)
    keys = acc[DH : 2 * DH].astype(BF16)
    values = acc[2 * DH :].astype(BF16)
    qkv_ref[0] = query
    qkv_ref[1] = keys
    qkv_ref[2] = values
    tail_w, head_w = tail_and_head(rate, events_ref, me * TOK)
    forward = pack(dot_wide_left(values.astype(F32) * tail_w, keys, NT))
    wait(o_copy)
    reverse = pack(dot_wide_left(query.astype(F32) * head_w, o_buf[...], NN))
    for d in range(N_SEQ):
        low = (jnp.minimum(me, d) + 1) * TOK
        high = jnp.maximum(me, d) * TOK
        count = jnp.float32(0.0)
        for k in range(events_ref.shape[0]):
            inside = (events_ref[k] >= low) & (events_ref[k] < high)
            count += jnp.where(inside, 1.0, 0.0)
        gap = jnp.maximum(high - low, 0).astype(F32)
        weight = jnp.exp(jnp.full((1, 128), -(rate * gap + DROP_LOGARITHM * count), F32))
        send_ref[d] = (jnp.where(d > me, forward, reverse) * weight).astype(BF16)


def local_kernel(rate_ref, events_ref, qkv_ref, o_ref, w_ref, grads_ref, half_ref):
    core = lax.axis_index("core")
    block = w_ref[...]
    for c in range(NC):
        mine = jnp.concatenate(
            [block[:, (y * NC + c) * OUT_ROWS : (y * NC + c + 1) * OUT_ROWS] for y in range(NY)],
            axis=1,
        )
        half_ref[lax.rem(core + c, NC)] = mine

    @pl.when(pl.program_id(0) == 0)
    def _():
        first = lax.axis_index("seq") * TOK
        rate = rate_ref[0]
        row = lax.broadcasted_iota(jnp.int32, (TOK, 1), 0)
        column = lax.broadcasted_iota(jnp.int32, (1, TOK), 1)
        later = row >= column
        gap = log_decay(rate, events_ref, first, row) - log_decay(rate, events_ref, first, column)
        weight = jnp.where(later, jnp.exp(jnp.where(later, gap, 0.0)), 0.0)
        query, keys, values, out = qkv_ref[0], qkv_ref[1], qkv_ref[2], o_ref[...]
        scores = dot(query, keys, TN) * weight
        dscores = dot(out, values, NN) * weight
        grads_ref[:DH] = dot_wide_right(keys, dscores, NT)
        grads_ref[DH : 2 * DH] = dot_wide_right(query, dscores, NN)
        grads_ref[2 * DH :] = dot_wide_right(out, scores, TN)


def weight_kernel(
    rate_ref, events_ref, got_ref, local_ref, qkv_ref, o_ref, x_ref, grads_ref, terms_ref,
    terms_buf, sems,
):
    me = lax.axis_index("seq")
    tail_w, head_w = tail_and_head(rate_ref[0], events_ref, me * TOK)
    prefix = jnp.zeros((PACK_ROWS, 128), F32)
    suffix = jnp.zeros((PACK_ROWS, 128), F32)
    for j in range(N_SEQ):
        state = got_ref[j].astype(F32)
        prefix += jnp.where(j < me, state, 0.0)
        suffix += jnp.where(j > me, state, 0.0)
    prefix, suffix = unpack(prefix), unpack(suffix)
    dquery = local_ref[:DH] + head_w * dot_wide_left(prefix, o_ref[...], TT)
    dkey = local_ref[DH : 2 * DH] + tail_w * dot_wide_left(suffix, qkv_ref[2], NN)
    dvalue = local_ref[2 * DH :] + tail_w * dot_wide_left(suffix, qkv_ref[1], TN)
    grads_ref[:DH] = (dquery * SCALE).astype(BF16)
    grads_ref[DH : 2 * DH] = dkey.astype(BF16)
    grads_ref[2 * DH :] = dvalue.astype(BF16)

    grads = grads_ref[...]
    sent = []
    for k in range(D // S_BLOCK):
        at = columns(k, S_BLOCK)
        terms_buf[:, at] = dot(grads, x_ref[:, at], NN).astype(BF16)
        copy = pltpu.make_async_copy(terms_buf.at[:, at], terms_ref.at[:, at], sems.at[k])
        copy.start()
        sent.append(copy)
    wait(sent)


def half_copies(w_ref, w_buf, sems, which):
    chunks = [columns(k, PER_X) for k in range(NX)]
    return fetch([(w_ref.at[which, :, at], w_buf.at[:, at]) for at in chunks], sems)


def give_kernel(grads_ref, w_ref, give_ref, w_buf, sems):
    grads = grads_ref[...]
    for k, copy in enumerate(half_copies(w_ref, w_buf, sems, 1)):
        wait([copy])
        give_ref[k] = dot(grads, w_buf[:, columns(k, PER_X)], TN).astype(BF16)


def keep_kernel(grads_ref, w_ref, taken_ref, sum_ref, w_buf, sems):
    grads = grads_ref[...]
    for k, copy in enumerate(half_copies(w_ref, w_buf, sems, 0)):
        wait([copy])
        mine = dot(grads, w_buf[:, columns(k, PER_X)], TN)
        sum_ref[k] = (mine + taken_ref[k].astype(F32)).astype(BF16)


def add_x_kernel(part_ref, out_ref):
    total = part_ref[0].astype(F32)
    for j in range(1, NX):
        total += part_ref[j].astype(F32)
    total = total.T.astype(BF16)
    for y in range(NY):
        out_ref[y] = total[y * OUT_ROWS : (y + 1) * OUT_ROWS]


def add_y_kernel(part_ref, out_ref):
    total = part_ref[0].astype(F32)
    for j in range(1, NY):
        total += part_ref[j].astype(F32)
    out_ref[...] = total.astype(BF16)


def square_kernel(summed_ref, out_ref, held_ref):
    held_ref[...] = summed_ref[...]
    summed = summed_ref[...].astype(F32)
    total = jnp.sum(jnp.sum(summed * summed, axis=0, keepdims=True), axis=1, keepdims=True)
    for j in range(N_SEQ):
        out_ref[j] = jnp.broadcast_to(total, (1, 128))


def sum_kernel(parts_ref, out_ref):
    total = parts_ref[0]
    for j in range(1, N_SEQ):
        total += parts_ref[j]
    out_ref[...] = jnp.broadcast_to(total, out_ref.shape)


def scale_kernel(parts_ref, summed_ref, out_ref):
    square = jnp.sum(parts_ref[...], axis=0, keepdims=True)[:, :1]
    limit = CLIP_RMS * math.sqrt(D * PARTS * N_TENSOR)
    factor = jnp.minimum(1.0, limit * lax.rsqrt(square + 1e-06))
    out_ref[...] = (summed_ref[...].astype(F32) * factor).astype(BF16)


SMEM = pl.BlockSpec(memory_space=pltpu.SMEM)
VMEM = pl.BlockSpec(memory_space=pltpu.VMEM)
HBM = pl.BlockSpec(memory_space=pltpu.HBM)
DMA = pltpu.SemaphoreType.DMA


def shape_of(shape, dtype=BF16):
    return jax.ShapeDtypeStruct(shape, dtype)


def call(kernel, in_specs, out_specs, out_shape, cost, scratch=(), limit=BIG, **grid):
    flops, moved = cost
    return pl.pallas_call(
        kernel,
        in_specs=in_specs,
        out_specs=out_specs,
        out_shape=out_shape,
        scratch_shapes=list(scratch),
        compiler_params=pltpu.CompilerParams(vmem_limit_bytes=limit),
        cost_estimate=pl.CostEstimate(flops=flops, bytes_accessed=moved, transcendentals=0),
        **grid,
    )


def project(rate, events, x, w, o):
    return call(
        project_kernel,
        [SMEM, SMEM, HBM, HBM, HBM],
        [VMEM, VMEM],
        [shape_of((3, DH, TOK)), shape_of((N_SEQ, PACK_ROWS, 128))],
        (2 * TOK * D * PARTS, 2 * D * (TOK + PARTS)),
        [
            pltpu.VMEM((TOK, D), BF16),
            pltpu.VMEM((PARTS, D), BF16),
            pltpu.VMEM((TOK, DH), BF16),
            pltpu.VMEM((PARTS, TOK), F32),
            DMA((2, D // K_BLOCK)),
            DMA((1,)),
        ],
    )(rate, events, x, w, o)


def local_part(rate, events, qkv, o, w):
    def whole(*shape):
        return pl.BlockSpec(shape, lambda i: (0,) * len(shape))

    return call(
        local_kernel,
        [
            SMEM,
            SMEM,
            whole(3, DH, TOK),
            whole(TOK, DH),
            pl.BlockSpec((PARTS, D // NX), lambda i: (0, i)),
        ],
        [whole(PARTS, TOK), pl.BlockSpec((NC, PARTS, PER_X), lambda i: (0, 0, i))],
        [shape_of((PARTS, TOK), F32), shape_of((NC, PARTS, HALF))],
        (20 * TOK * TOK * DH, 4 * D * PARTS),
        limit=MIDDLE,
        grid=(NX,),
    )(rate, events, qkv, o, w)


def weight_terms(rate, events, got, local, qkv, o, x):
    return call(
        weight_kernel,
        [SMEM, SMEM, VMEM, VMEM, VMEM, VMEM, VMEM],
        [VMEM, HBM],
        [shape_of((PARTS, TOK)), shape_of((PARTS, D))],
        (2 * TOK * D * PARTS, 2 * D * (TOK + PARTS)),
        [
            pltpu.VMEM((PARTS, D), BF16),
            DMA((D // S_BLOCK,)),
        ],
        limit=MIDDLE,
    )(rate, events, got, local, qkv, o, x)


def give_part(grads, halves):
    return call(
        give_kernel,
        [VMEM, HBM],
        VMEM,
        shape_of((NX, TOK, PER_X)),
        (TOK * D * PARTS, D * (TOK + PARTS)),
        [pltpu.VMEM((PARTS, HALF), BF16), DMA((NX,))],
        limit=MIDDLE,
    )(grads, halves)


def keep_part(grads, halves, taken):
    return call(
        keep_kernel,
        [VMEM, HBM, VMEM],
        VMEM,
        shape_of((NX, TOK, PER_X)),
        (TOK * D * PARTS, D * (2 * TOK + PARTS)),
        [pltpu.VMEM((PARTS, HALF), BF16), DMA((NX,))],
        limit=MIDDLE,
    )(grads, halves, taken)


def add_x(parts):
    shape = (NY, OUT_ROWS, TOK)
    return call(
        add_x_kernel, [VMEM], VMEM, shape_of(shape), (4 * parts.size, 4 * parts.size), limit=SMALL
    )(parts)


def add_y(parts):
    shape = (OUT_ROWS, TOK)
    return call(
        add_y_kernel, [VMEM], VMEM, shape_of(shape), (parts.size, 2 * parts.size), limit=SMALL
    )(parts)


def square_of(summed):
    return call(
        square_kernel,
        [VMEM],
        [VMEM, VMEM],
        [shape_of((N_SEQ, 1, 128), F32), shape_of(summed.shape)],
        (2 * summed.size, 2 * summed.size),
        limit=SMALL,
    )(summed)


def sum_of(parts):
    return call(
        sum_kernel, [VMEM], VMEM, shape_of((N_TENSOR, 128), F32), (parts.size, 4 * parts.size), limit=SMALL
    )(parts)


def scaled(parts, summed):
    return call(
        scale_kernel,
        [VMEM, VMEM],
        VMEM,
        shape_of(summed.shape),
        (2 * summed.size, 4 * summed.size),
        limit=SMALL,
    )(parts, summed)


def body(layer_inputs, projection_matrices, result_sensitivity, channel_fading_rate, loss_events):
    x, o, rate, events = layer_inputs, result_sensitivity, channel_fading_rate, loss_events
    w = projection_matrices.transpose(1, 2, 0).reshape(PARTS, D)
    qkv, send = project(rate, events, x, w, o)
    got = lax.all_to_all(send, "seq", 0, 0, tiled=True)
    local, halves = local_part(rate, events, qkv, o, w)
    grads, terms = weight_terms(rate, events, got, local, qkv, o, x)
    summed = lax.psum_scatter(terms, "seq", scatter_dimension=1, tiled=True)

    give = give_part(grads, halves)
    taken = lax.ppermute(give, "core", [(0, 1), (1, 0)])
    part = keep_part(grads, halves, taken)
    part = add_x(lax.all_to_all(part, "x", 0, 0, tiled=True))
    input_grad = add_y(lax.all_to_all(part, "y", 0, 0, tiled=True))

    summed, input_grad = lax.optimization_barrier((summed, input_grad))
    square, summed = square_of(summed)
    square = lax.all_to_all(square, "seq", 0, 0, tiled=True)
    square = lax.all_to_all(sum_of(square), TENSOR, 0, 0, tiled=True)
    weight_grad = scaled(square, summed)
    return (input_grad, weight_grad.reshape(3, DH, D // N_SEQ).transpose(2, 0, 1))


def solution(mesh):
    fine = Mesh(mesh.devices.reshape(N_SEQ, NX, NY, NC), ("seq",) + TENSOR)
    return jax.shard_map(
        body,
        mesh=fine,
        in_specs=(P("seq", None), P(None, None, TENSOR), P("seq", TENSOR), P(TENSOR), P()),
        out_specs=(P(TENSOR, "seq"), P("seq", None, TENSOR)),
        check_vma=False,
    )
```

```python
import math

import jax
import jax.numpy as jnp
from jax import lax
from jax.experimental import pallas as pl
from jax.experimental.pallas import tpu as pltpu
from jax.sharding import Mesh, PartitionSpec as P

DH = 96
TOK = 192
D = 6144
N_SEQ = 12
NX, NY, NC = 4, 8, 2
N_TENSOR = NX * NY * NC
OUT_ROWS = D // N_TENSOR
HALF = D // NC
PER_X = HALF // NX
PARTS = 3 * DH
K_BLOCK = 1536
S_BLOCK = 1536
PACK_ROWS = 72
PACK_REST = 32
BIG = 60 << 20
MIDDLE = 50 << 20
SMALL = 8 << 20

DROP_LOGARITHM = 0.3
CLIP_RMS = 0.5
SCALE = DH ** (-0.5)
F32 = jnp.float32
BF16 = jnp.bfloat16
TENSOR = ("x", "y", "core")

NN = (((1,), (0,)), ((), ()))
NT = (((1,), (1,)), ((), ()))
TN = (((0,), (0,)), ((), ()))
TT = (((0,), (1,)), ((), ()))


def dot(a, b, dims):
    return lax.dot_general(a, b, dims, preferred_element_type=F32)


def split(a):
    high = a.astype(BF16)
    return high, (a - high.astype(F32)).astype(BF16)


def dot_wide_left(a, b, dims):
    high, low = split(a)
    return dot(high, b, dims) + dot(low, b, dims)


def dot_wide_right(a, b, dims):
    high, low = split(b)
    return dot(a, high, dims) + dot(a, low, dims)


def log_decay(rate, events, first, steps):
    seen = jnp.zeros(steps.shape, F32)
    for k in range(events.shape[0]):
        place = events[k] - first
        seen += jnp.where((steps >= place) & (place >= 0), 1.0, 0.0)
    return -(rate * (steps + 1).astype(F32) + DROP_LOGARITHM * seen)


def tail_and_head(rate, events, first):
    steps = lax.broadcasted_iota(jnp.int32, (1, TOK), 1)
    cumul = log_decay(rate, events, first, steps)
    total = log_decay(rate, events, first, jnp.full((1, 1), TOK - 1, jnp.int32))
    return jnp.exp(total - cumul), jnp.exp(cumul)


def pack(state):
    rest = [state[PACK_ROWS:, k * PACK_REST : (k + 1) * PACK_REST] for k in range(DH // PACK_REST)]
    return jnp.concatenate([state[:PACK_ROWS], jnp.concatenate(rest, axis=0)], axis=1)


def unpack(packed):
    rows = DH - PACK_ROWS
    rest = [packed[k * rows : (k + 1) * rows, DH:] for k in range(DH // PACK_REST)]
    return jnp.concatenate([packed[:, :DH], jnp.concatenate(rest, axis=1)], axis=0)


def columns(k, size):
    return pl.ds(k * size, size)


def fetch(pairs, sems):
    copies = [pltpu.make_async_copy(a, b, sems.at[k]) for k, (a, b) in enumerate(pairs)]
    for copy in copies:
        copy.start()
    return copies


def wait(copies):
    for copy in copies:
        copy.wait()


def project_kernel(
    rate_ref, events_ref, x_ref, w_ref, o_ref, qkv_ref, send_ref,
    x_buf, w_buf, o_buf, acc, sems, o_sem,
):
    copies = []
    for k in range(D // K_BLOCK):
        at = columns(k, K_BLOCK)
        pair = (
            pltpu.make_async_copy(x_ref.at[:, at], x_buf.at[:, at], sems.at[0, k]),
            pltpu.make_async_copy(w_ref.at[:, at], w_buf.at[:, at], sems.at[1, k]),
        )
        for copy in pair:
            copy.start()
        copies.append(pair)
    o_copy = fetch([(o_ref, o_buf)], o_sem)
    for k, pair in enumerate(copies):
        wait(pair)
        at = columns(k, K_BLOCK)
        term = dot(w_buf[:, at], x_buf[:, at], NT)
        if k == 0:
            acc[...] = term
        else:
            acc[...] += term

    me = lax.axis_index("seq")
    rate = rate_ref[0]
    query = (acc[:DH] * SCALE).astype(BF16)
    keys = acc[DH : 2 * DH].astype(BF16)
    values = acc[2 * DH :].astype(BF16)
    qkv_ref[0] = query
    qkv_ref[1] = keys
    qkv_ref[2] = values
    tail_w, head_w = tail_and_head(rate, events_ref, me * TOK)
    forward = pack(dot_wide_left(values.astype(F32) * tail_w, keys, NT))
    wait(o_copy)
    reverse = pack(dot_wide_left(query.astype(F32) * head_w, o_buf[...], NN))
    for d in range(N_SEQ):
        low = (jnp.minimum(me, d) + 1) * TOK
        high = jnp.maximum(me, d) * TOK
        count = jnp.float32(0.0)
        for k in range(events_ref.shape[0]):
            inside = (events_ref[k] >= low) & (events_ref[k] < high)
            count += jnp.where(inside, 1.0, 0.0)
        gap = jnp.maximum(high - low, 0).astype(F32)
        weight = jnp.exp(jnp.full((1, 128), -(rate * gap + DROP_LOGARITHM * count), F32))
        send_ref[d] = (jnp.where(d > me, forward, reverse) * weight).astype(BF16)


def local_kernel(rate_ref, events_ref, qkv_ref, o_ref, x_ref, grads_ref, x_buf, x_sem):
    x_copy = fetch([(x_ref, x_buf)], x_sem)
    first = lax.axis_index("seq") * TOK
    rate = rate_ref[0]
    row = lax.broadcasted_iota(jnp.int32, (TOK, 1), 0)
    column = lax.broadcasted_iota(jnp.int32, (1, TOK), 1)
    later = row >= column
    gap = log_decay(rate, events_ref, first, row) - log_decay(rate, events_ref, first, column)
    weight = jnp.where(later, jnp.exp(jnp.where(later, gap, 0.0)), 0.0)
    query, keys, values, out = qkv_ref[0], qkv_ref[1], qkv_ref[2], o_ref[...]
    scores = dot(query, keys, TN) * weight
    dscores = dot(out, values, NN) * weight
    grads_ref[:DH] = dot_wide_right(keys, dscores, NT)
    grads_ref[DH : 2 * DH] = dot_wide_right(query, dscores, NN)
    grads_ref[2 * DH :] = dot_wide_right(out, scores, TN)
    wait(x_copy)


def weight_kernel(
    rate_ref, events_ref, got_ref, local_ref, qkv_ref, o_ref, x_ref, grads_ref, terms_ref,
    terms_buf, sems,
):
    me = lax.axis_index("seq")
    tail_w, head_w = tail_and_head(rate_ref[0], events_ref, me * TOK)
    prefix = jnp.zeros((PACK_ROWS, 128), F32)
    suffix = jnp.zeros((PACK_ROWS, 128), F32)
    for j in range(N_SEQ):
        state = got_ref[j].astype(F32)
        prefix += jnp.where(j < me, state, 0.0)
        suffix += jnp.where(j > me, state, 0.0)
    prefix, suffix = unpack(prefix), unpack(suffix)
    dquery = local_ref[:DH] + head_w * dot_wide_left(prefix, o_ref[...], TT)
    dkey = local_ref[DH : 2 * DH] + tail_w * dot_wide_left(suffix, qkv_ref[2], NN)
    dvalue = local_ref[2 * DH :] + tail_w * dot_wide_left(suffix, qkv_ref[1], TN)
    grads_ref[:DH] = (dquery * SCALE).astype(BF16)
    grads_ref[DH : 2 * DH] = dkey.astype(BF16)
    grads_ref[2 * DH :] = dvalue.astype(BF16)

    grads = grads_ref[...]
    sent = []
    for k in range(D // S_BLOCK):
        at = columns(k, S_BLOCK)
        terms_buf[:, at] = dot(grads, x_ref[:, at], NN).astype(BF16)
        copy = pltpu.make_async_copy(terms_buf.at[:, at], terms_ref.at[:, at], sems.at[k])
        copy.start()
        sent.append(copy)
    wait(sent)


def fetch_w(w_ref, w_buf, sems):
    chunks = [columns(k, D // NX) for k in range(NX)]
    return fetch([(w_ref.at[:, at], w_buf.at[:, at]) for at in chunks], sems)


def core_columns(w_buf, k, c):
    starts = [k * (D // NX) + (y * NC + c) * OUT_ROWS for y in range(NY)]
    return jnp.concatenate([w_buf[:, at : at + OUT_ROWS] for at in starts], axis=1)


def give_kernel(grads_ref, w_ref, give_ref, w_buf, sems):
    core = lax.axis_index("core")
    grads = grads_ref[...]
    for k, copy in enumerate(fetch_w(w_ref, w_buf, sems)):
        wait([copy])
        for c in range(NC):

            @pl.when(core != c)
            def _():
                give_ref[k] = dot(grads, core_columns(w_buf, k, c), TN).astype(BF16)


def keep_kernel(grads_ref, w_ref, taken_ref, sum_ref, w_buf, sems):
    core = lax.axis_index("core")
    grads = grads_ref[...]
    for k, copy in enumerate(fetch_w(w_ref, w_buf, sems)):
        wait([copy])
        for c in range(NC):

            @pl.when(core == c)
            def _():
                mine = dot(grads, core_columns(w_buf, k, c), TN)
                sum_ref[k] = (mine + taken_ref[k].astype(F32)).astype(BF16)


def add_x_kernel(part_ref, out_ref):
    total = part_ref[0].astype(F32)
    for j in range(1, NX):
        total += part_ref[j].astype(F32)
    total = total.T.astype(BF16)
    for y in range(NY):
        out_ref[y] = total[y * OUT_ROWS : (y + 1) * OUT_ROWS]


def add_y_kernel(part_ref, out_ref):
    total = part_ref[0].astype(F32)
    for j in range(1, NY):
        total += part_ref[j].astype(F32)
    out_ref[...] = total.astype(BF16)


def square_kernel(summed_ref, out_ref, held_ref):
    held_ref[...] = summed_ref[...]
    summed = summed_ref[...].astype(F32)
    total = jnp.sum(jnp.sum(summed * summed, axis=0, keepdims=True), axis=1, keepdims=True)
    out_ref[...] = jnp.broadcast_to(total, out_ref.shape)


def sum_kernel(parts_ref, out_ref):
    total = jnp.sum(parts_ref[...], axis=0, keepdims=True)
    for j in range(N_SEQ):
        out_ref[j] = total


def scale_kernel(parts_ref, summed_ref, out_ref):
    square = parts_ref[0]
    for j in range(1, N_SEQ):
        square += parts_ref[j]
    square = square[:, :1]
    limit = CLIP_RMS * math.sqrt(D * PARTS * N_TENSOR)
    factor = jnp.minimum(1.0, limit * lax.rsqrt(square + 1e-06))
    out_ref[...] = (summed_ref[...].astype(F32) * factor).astype(BF16)


SMEM = pl.BlockSpec(memory_space=pltpu.SMEM)
VMEM = pl.BlockSpec(memory_space=pltpu.VMEM)
HBM = pl.BlockSpec(memory_space=pltpu.HBM)
DMA = pltpu.SemaphoreType.DMA


def shape_of(shape, dtype=BF16):
    return jax.ShapeDtypeStruct(shape, dtype)


def call(kernel, in_specs, out_specs, out_shape, cost, scratch=(), limit=BIG, **grid):
    flops, moved = cost
    return pl.pallas_call(
        kernel,
        in_specs=in_specs,
        out_specs=out_specs,
        out_shape=out_shape,
        scratch_shapes=list(scratch),
        compiler_params=pltpu.CompilerParams(vmem_limit_bytes=limit),
        cost_estimate=pl.CostEstimate(flops=flops, bytes_accessed=moved, transcendentals=0),
        **grid,
    )


def project(rate, events, x, w, o):
    return call(
        project_kernel,
        [SMEM, SMEM, HBM, HBM, HBM],
        [VMEM, VMEM],
        [shape_of((3, DH, TOK)), shape_of((N_SEQ, PACK_ROWS, 128))],
        (2 * TOK * D * PARTS, 2 * D * (TOK + PARTS)),
        [
            pltpu.VMEM((TOK, D), BF16),
            pltpu.VMEM((PARTS, D), BF16),
            pltpu.VMEM((TOK, DH), BF16),
            pltpu.VMEM((PARTS, TOK), F32),
            DMA((2, D // K_BLOCK)),
            DMA((1,)),
        ],
    )(rate, events, x, w, o)


def local_part(rate, events, qkv, o, x):
    return call(
        local_kernel,
        [SMEM, SMEM, VMEM, VMEM, HBM],
        [VMEM, VMEM],
        [shape_of((PARTS, TOK), F32), shape_of((TOK, D))],
        (20 * TOK * TOK * DH, 8 * TOK * PARTS + 2 * TOK * D),
        [DMA((1,))],
        limit=MIDDLE,
    )(rate, events, qkv, o, x)


def weight_terms(rate, events, got, local, qkv, o, x):
    return call(
        weight_kernel,
        [SMEM, SMEM, VMEM, VMEM, VMEM, VMEM, VMEM],
        [VMEM, HBM],
        [shape_of((PARTS, TOK)), shape_of((PARTS, D))],
        (2 * TOK * D * PARTS, 2 * D * (TOK + PARTS)),
        [
            pltpu.VMEM((PARTS, D), BF16),
            DMA((D // S_BLOCK,)),
        ],
        limit=MIDDLE,
    )(rate, events, got, local, qkv, o, x)


def give_part(grads, w):
    return call(
        give_kernel,
        [VMEM, HBM],
        VMEM,
        shape_of((NX, TOK, PER_X)),
        (TOK * D * PARTS, D * (TOK + PARTS)),
        [pltpu.VMEM((PARTS, D), BF16), DMA((NX,))],
        limit=MIDDLE,
    )(grads, w)


def keep_part(grads, w, taken):
    return call(
        keep_kernel,
        [VMEM, HBM, VMEM],
        VMEM,
        shape_of((NX, TOK, PER_X)),
        (TOK * D * PARTS, D * (2 * TOK + PARTS)),
        [pltpu.VMEM((PARTS, D), BF16), DMA((NX,))],
        limit=MIDDLE,
    )(grads, w, taken)


def add_x(parts):
    shape = (NY, OUT_ROWS, TOK)
    return call(
        add_x_kernel, [VMEM], VMEM, shape_of(shape), (4 * parts.size, 4 * parts.size), limit=SMALL
    )(parts)


def add_y(parts):
    shape = (OUT_ROWS, TOK)
    return call(
        add_y_kernel, [VMEM], VMEM, shape_of(shape), (parts.size, 2 * parts.size), limit=SMALL
    )(parts)


def square_of(summed):
    return call(
        square_kernel,
        [VMEM],
        [VMEM, VMEM],
        [shape_of((N_TENSOR, 128), F32), shape_of(summed.shape)],
        (2 * summed.size, 2 * summed.size),
        limit=SMALL,
    )(summed)


def sum_of(parts):
    return call(
        sum_kernel, [VMEM], VMEM, shape_of((N_SEQ, 1, 128), F32), (parts.size, 4 * parts.size), limit=SMALL
    )(parts)


def scaled(parts, summed):
    return call(
        scale_kernel,
        [VMEM, VMEM],
        VMEM,
        shape_of(summed.shape),
        (2 * summed.size, 4 * summed.size),
        limit=SMALL,
    )(parts, summed)


def body(layer_inputs, projection_matrices, result_sensitivity, channel_fading_rate, loss_events):
    x, o, rate, events = layer_inputs, result_sensitivity, channel_fading_rate, loss_events
    w = projection_matrices.transpose(1, 2, 0).reshape(PARTS, D)
    qkv, send = project(rate, events, x, w, o)
    got = lax.all_to_all(send, "seq", 0, 0, tiled=True)
    local, x = local_part(rate, events, qkv, o, x)
    grads, terms = weight_terms(rate, events, got, local, qkv, o, x)
    summed = lax.psum_scatter(terms, "seq", scatter_dimension=1, tiled=True)

    give = give_part(grads, w)
    taken = lax.ppermute(give, "core", [(0, 1), (1, 0)])
    part = keep_part(grads, w, taken)
    part = add_x(lax.all_to_all(part, "x", 0, 0, tiled=True))
    input_grad = add_y(lax.all_to_all(part, "y", 0, 0, tiled=True))

    summed, input_grad = lax.optimization_barrier((summed, input_grad))
    square, summed = square_of(summed)
    square = lax.all_to_all(square, TENSOR, 0, 0, tiled=True)
    square = lax.all_to_all(sum_of(square), "seq", 0, 0, tiled=True)
    weight_grad = scaled(square, summed)
    return (input_grad, weight_grad.reshape(3, DH, D // N_SEQ).transpose(2, 0, 1))


def solution(mesh):
    fine = Mesh(mesh.devices.reshape(N_SEQ, NX, NY, NC), ("seq",) + TENSOR)
    return jax.shard_map(
        body,
        mesh=fine,
        in_specs=(P("seq", None), P(None, None, TENSOR), P("seq", TENSOR), P(TENSOR), P()),
        out_specs=(P(TENSOR, "seq"), P("seq", None, TENSOR)),
        check_vma=False,
    )
```

```python
import math

import jax
import jax.numpy as jnp
from jax import lax
from jax.experimental import pallas as pl
from jax.experimental.pallas import tpu as pltpu
from jax.sharding import Mesh, PartitionSpec as P

DH = 96
TOK = 192
D = 6144
N_SEQ = 12
NX, NY, NC = 4, 8, 2
N_TENSOR = NX * NY * NC
OUT_ROWS = D // N_TENSOR
HALF = D // NC
PER_X = HALF // NX
PARTS = 3 * DH
K_BLOCK = 2048
S_CHUNKS = (512, 1024, 1536, 1536, 1536)
PACK_ROWS = 72
PACK_REST = 32
BIG = 60 << 20
MIDDLE = 50 << 20
SMALL = 8 << 20

DROP_LOGARITHM = 0.3
CLIP_RMS = 0.5
SCALE = DH ** (-0.5)
F32 = jnp.float32
BF16 = jnp.bfloat16
TENSOR = ("x", "y", "core")

NN = (((1,), (0,)), ((), ()))
NT = (((1,), (1,)), ((), ()))
TN = (((0,), (0,)), ((), ()))


def dot(a, b, dims):
    return lax.dot_general(a, b, dims, preferred_element_type=F32)


def split(a):
    high = a.astype(BF16)
    return high, (a - high.astype(F32)).astype(BF16)


def dot_wide_left(a, b, dims):
    high, low = split(a)
    return dot(high, b, dims) + dot(low, b, dims)


def dot_wide_right(a, b, dims):
    high, low = split(b)
    return dot(a, high, dims) + dot(a, low, dims)


def log_decay(rate, events, first, steps):
    seen = jnp.zeros(steps.shape, F32)
    for k in range(events.shape[0]):
        place = events[k] - first
        seen += jnp.where((steps >= place) & (place >= 0), 1.0, 0.0)
    return -(rate * (steps + 1).astype(F32) + DROP_LOGARITHM * seen)


def tail_and_head(rate, events, first):
    steps = lax.broadcasted_iota(jnp.int32, (1, TOK), 1)
    cumul = log_decay(rate, events, first, steps)
    total = log_decay(rate, events, first, jnp.full((1, 1), TOK - 1, jnp.int32))
    return jnp.exp(total - cumul), jnp.exp(cumul)


def pack(state):
    rest = [state[PACK_ROWS:, k * PACK_REST : (k + 1) * PACK_REST] for k in range(DH // PACK_REST)]
    return jnp.concatenate([state[:PACK_ROWS], jnp.concatenate(rest, axis=0)], axis=1)


def unpack(packed):
    rows = DH - PACK_ROWS
    rest = [packed[k * rows : (k + 1) * rows, DH:] for k in range(DH // PACK_REST)]
    return jnp.concatenate([packed[:, :DH], jnp.concatenate(rest, axis=1)], axis=0)


def columns(k, size):
    return pl.ds(k * size, size)


def fetch(pairs, sems):
    copies = [pltpu.make_async_copy(a, b, sems.at[k]) for k, (a, b) in enumerate(pairs)]
    for copy in copies:
        copy.start()
    return copies


def wait(copies):
    for copy in copies:
        copy.wait()


def project_kernel(
    rate_ref, events_ref, x_ref, w_ref, o_ref, qkv_ref, send_ref,
    x_buf, w_buf, o_buf, acc, sems, o_sem,
):
    copies = []
    for k in range(D // K_BLOCK):
        at = columns(k, K_BLOCK)
        pair = (
            pltpu.make_async_copy(x_ref.at[:, at], x_buf.at[:, at], sems.at[0, k]),
            pltpu.make_async_copy(w_ref.at[:, at], w_buf.at[:, at], sems.at[1, k]),
        )
        for copy in pair:
            copy.start()
        copies.append(pair)
    o_copy = fetch([(o_ref, o_buf)], o_sem)
    for k, pair in enumerate(copies):
        wait(pair)
        at = columns(k, K_BLOCK)
        term = dot(w_buf[:, at], x_buf[:, at], NT)
        if k == 0:
            acc[...] = term
        else:
            acc[...] += term

    me = lax.axis_index("seq")
    rate = rate_ref[0]
    query = (acc[:DH] * SCALE).astype(BF16)
    keys = acc[DH : 2 * DH].astype(BF16)
    values = acc[2 * DH :].astype(BF16)
    qkv_ref[0] = query
    qkv_ref[1] = keys
    qkv_ref[2] = values
    tail_w, head_w = tail_and_head(rate, events_ref, me * TOK)
    forward = pack(dot_wide_left(values.astype(F32) * tail_w, keys, NT))
    wait(o_copy)
    reverse = pack(dot_wide_left(query.astype(F32) * head_w, o_buf[...], NN))
    for d in range(N_SEQ):
        low = (jnp.minimum(me, d) + 1) * TOK
        high = jnp.maximum(me, d) * TOK
        count = jnp.float32(0.0)
        for k in range(events_ref.shape[0]):
            inside = (events_ref[k] >= low) & (events_ref[k] < high)
            count += jnp.where(inside, 1.0, 0.0)
        gap = jnp.maximum(high - low, 0).astype(F32)
        weight = jnp.exp(jnp.full((1, 128), -(rate * gap + DROP_LOGARITHM * count), F32))
        send_ref[d] = (jnp.where(d > me, forward, reverse) * weight).astype(BF16)


def local_kernel(rate_ref, events_ref, qkv_ref, o_ref, x_ref, grads_ref, x_buf, turned_ref, x_sem):
    x_copy = fetch([(x_ref, x_buf)], x_sem)
    first = lax.axis_index("seq") * TOK
    rate = rate_ref[0]
    row = lax.broadcasted_iota(jnp.int32, (TOK, 1), 0)
    column = lax.broadcasted_iota(jnp.int32, (1, TOK), 1)
    later = row >= column
    gap = log_decay(rate, events_ref, first, row) - log_decay(rate, events_ref, first, column)
    weight = jnp.where(later, jnp.exp(jnp.where(later, gap, 0.0)), 0.0)
    query, keys, values, out = qkv_ref[0], qkv_ref[1], qkv_ref[2], o_ref[...]
    scores = dot(query, keys, TN) * weight
    dscores = dot(out, values, NN) * weight
    grads_ref[:DH] = dot_wide_right(keys, dscores, NT)
    grads_ref[DH : 2 * DH] = dot_wide_right(query, dscores, NN)
    grads_ref[2 * DH :] = dot_wide_right(out, scores, TN)
    turned_ref[...] = out.astype(F32).T.astype(BF16)
    wait(x_copy)


def weight_kernel(
    rate_ref, events_ref, got_ref, local_ref, qkv_ref, o_ref, x_ref, grads_ref, terms_ref,
    terms_buf, sems,
):
    me = lax.axis_index("seq")
    tail_w, head_w = tail_and_head(rate_ref[0], events_ref, me * TOK)
    prefix = jnp.zeros((PACK_ROWS, 128), F32)
    suffix = jnp.zeros((PACK_ROWS, 128), F32)
    for j in range(N_SEQ):
        state = got_ref[j].astype(F32)
        prefix += jnp.where(j < me, state, 0.0)
        suffix += jnp.where(j > me, state, 0.0)
    prefix, suffix = unpack(prefix), unpack(suffix)
    dquery = local_ref[:DH] + head_w * dot_wide_left(prefix, o_ref[...], TN)
    dkey = local_ref[DH : 2 * DH] + tail_w * dot_wide_left(suffix, qkv_ref[2], NN)
    dvalue = local_ref[2 * DH :] + tail_w * dot_wide_left(suffix, qkv_ref[1], TN)
    grads_ref[:DH] = (dquery * SCALE).astype(BF16)
    grads_ref[DH : 2 * DH] = dkey.astype(BF16)
    grads_ref[2 * DH :] = dvalue.astype(BF16)

    grads = grads_ref[...]
    sent = []
    start = 0
    for k, size in enumerate(S_CHUNKS):
        at = pl.ds(start, size)
        start += size
        terms_buf[:, at] = dot(grads, x_ref[:, at], NN).astype(BF16)
        copy = pltpu.make_async_copy(terms_buf.at[:, at], terms_ref.at[:, at], sems.at[k])
        copy.start()
        sent.append(copy)
    wait(sent)


def fetch_w(w_ref, w_buf, sems):
    chunks = [columns(k, D // NX) for k in range(NX)]
    return fetch([(w_ref.at[:, at], w_buf.at[:, at]) for at in chunks], sems)


def core_columns(w_buf, k, c):
    starts = [k * (D // NX) + (y * NC + c) * OUT_ROWS for y in range(NY)]
    return jnp.concatenate([w_buf[:, at : at + OUT_ROWS] for at in starts], axis=1)


def give_kernel(grads_ref, w_ref, give_ref, w_buf, sems):
    core = lax.axis_index("core")
    grads = grads_ref[...]
    for k, copy in enumerate(fetch_w(w_ref, w_buf, sems)):
        wait([copy])
        for c in range(NC):

            @pl.when(core != c)
            def _():
                give_ref[k] = dot(grads, core_columns(w_buf, k, c), TN).astype(BF16)


def keep_kernel(grads_ref, w_ref, taken_ref, sum_ref, w_buf, sems):
    core = lax.axis_index("core")
    grads = grads_ref[...]
    for k, copy in enumerate(fetch_w(w_ref, w_buf, sems)):
        wait([copy])
        for c in range(NC):

            @pl.when(core == c)
            def _():
                mine = dot(grads, core_columns(w_buf, k, c), TN)
                sum_ref[k] = (mine + taken_ref[k].astype(F32)).astype(BF16)


def add_x_kernel(part_ref, out_ref):
    total = part_ref[0].astype(F32)
    for j in range(1, NX):
        total += part_ref[j].astype(F32)
    total = total.T.astype(BF16)
    for y in range(NY):
        out_ref[y] = total[y * OUT_ROWS : (y + 1) * OUT_ROWS]


def add_y_kernel(part_ref, out_ref):
    total = part_ref[0].astype(F32)
    for j in range(1, NY):
        total += part_ref[j].astype(F32)
    out_ref[...] = total.astype(BF16)


def square_kernel(summed_ref, out_ref, held_ref):
    held_ref[...] = summed_ref[...]
    summed = summed_ref[...].astype(F32)
    total = jnp.sum(jnp.sum(summed * summed, axis=0, keepdims=True), axis=1, keepdims=True)
    out_ref[...] = jnp.broadcast_to(total, out_ref.shape)


def sum_kernel(parts_ref, out_ref):
    total = jnp.sum(parts_ref[...], axis=0, keepdims=True)
    for j in range(N_SEQ):
        out_ref[j] = total


def scale_kernel(parts_ref, summed_ref, out_ref):
    square = parts_ref[0]
    for j in range(1, N_SEQ):
        square += parts_ref[j]
    square = square[:, :1]
    limit = CLIP_RMS * math.sqrt(D * PARTS * N_TENSOR)
    factor = jnp.minimum(1.0, limit * lax.rsqrt(square + 1e-06))
    out_ref[...] = (summed_ref[...].astype(F32) * factor).astype(BF16)


SMEM = pl.BlockSpec(memory_space=pltpu.SMEM)
VMEM = pl.BlockSpec(memory_space=pltpu.VMEM)
HBM = pl.BlockSpec(memory_space=pltpu.HBM)
DMA = pltpu.SemaphoreType.DMA


def shape_of(shape, dtype=BF16):
    return jax.ShapeDtypeStruct(shape, dtype)


def call(kernel, in_specs, out_specs, out_shape, cost, scratch=(), limit=BIG, **grid):
    flops, moved = cost
    return pl.pallas_call(
        kernel,
        in_specs=in_specs,
        out_specs=out_specs,
        out_shape=out_shape,
        scratch_shapes=list(scratch),
        compiler_params=pltpu.CompilerParams(vmem_limit_bytes=limit),
        cost_estimate=pl.CostEstimate(flops=flops, bytes_accessed=moved, transcendentals=0),
        **grid,
    )


def project(rate, events, x, w, o):
    return call(
        project_kernel,
        [SMEM, SMEM, HBM, HBM, HBM],
        [VMEM, VMEM],
        [shape_of((3, DH, TOK)), shape_of((N_SEQ, PACK_ROWS, 128))],
        (2 * TOK * D * PARTS, 2 * D * (TOK + PARTS)),
        [
            pltpu.VMEM((TOK, D), BF16),
            pltpu.VMEM((PARTS, D), BF16),
            pltpu.VMEM((TOK, DH), BF16),
            pltpu.VMEM((PARTS, TOK), F32),
            DMA((2, D // K_BLOCK)),
            DMA((1,)),
        ],
    )(rate, events, x, w, o)


def local_part(rate, events, qkv, o, x):
    return call(
        local_kernel,
        [SMEM, SMEM, VMEM, VMEM, HBM],
        [VMEM, VMEM, VMEM],
        [shape_of((PARTS, TOK), F32), shape_of((TOK, D)), shape_of((DH, TOK))],
        (20 * TOK * TOK * DH, 8 * TOK * PARTS + 2 * TOK * D),
        [DMA((1,))],
        limit=MIDDLE,
    )(rate, events, qkv, o, x)


def weight_terms(rate, events, got, local, qkv, o, x):
    return call(
        weight_kernel,
        [SMEM, SMEM, VMEM, VMEM, VMEM, VMEM, VMEM],
        [VMEM, HBM],
        [shape_of((PARTS, TOK)), shape_of((PARTS, D))],
        (2 * TOK * D * PARTS, 2 * D * (TOK + PARTS)),
        [
            pltpu.VMEM((PARTS, D), BF16),
            DMA((len(S_CHUNKS),)),
        ],
        limit=MIDDLE,
    )(rate, events, got, local, qkv, o, x)


def give_part(grads, w):
    return call(
        give_kernel,
        [VMEM, HBM],
        VMEM,
        shape_of((NX, TOK, PER_X)),
        (TOK * D * PARTS, D * (TOK + PARTS)),
        [pltpu.VMEM((PARTS, D), BF16), DMA((NX,))],
        limit=MIDDLE,
    )(grads, w)


def keep_part(grads, w, taken):
    return call(
        keep_kernel,
        [VMEM, HBM, VMEM],
        VMEM,
        shape_of((NX, TOK, PER_X)),
        (TOK * D * PARTS, D * (2 * TOK + PARTS)),
        [pltpu.VMEM((PARTS, D), BF16), DMA((NX,))],
        limit=MIDDLE,
    )(grads, w, taken)


def add_x(parts):
    shape = (NY, OUT_ROWS, TOK)
    return call(
        add_x_kernel, [VMEM], VMEM, shape_of(shape), (4 * parts.size, 4 * parts.size), limit=SMALL
    )(parts)


def add_y(parts):
    shape = (OUT_ROWS, TOK)
    return call(
        add_y_kernel, [VMEM], VMEM, shape_of(shape), (parts.size, 2 * parts.size), limit=SMALL
    )(parts)


def square_of(summed):
    return call(
        square_kernel,
        [VMEM],
        [VMEM, VMEM],
        [shape_of((N_TENSOR, 128), F32), shape_of(summed.shape)],
        (2 * summed.size, 2 * summed.size),
        limit=SMALL,
    )(summed)


def sum_of(parts):
    return call(
        sum_kernel, [VMEM], VMEM, shape_of((N_SEQ, 1, 128), F32), (parts.size, 4 * parts.size), limit=SMALL
    )(parts)


def scaled(parts, summed):
    return call(
        scale_kernel,
        [VMEM, VMEM],
        VMEM,
        shape_of(summed.shape),
        (2 * summed.size, 4 * summed.size),
        limit=SMALL,
    )(parts, summed)


def body(layer_inputs, projection_matrices, result_sensitivity, channel_fading_rate, loss_events):
    x, o, rate, events = layer_inputs, result_sensitivity, channel_fading_rate, loss_events
    w = projection_matrices.transpose(1, 2, 0).reshape(PARTS, D)
    qkv, send = project(rate, events, x, w, o)
    got = lax.all_to_all(send, "seq", 0, 0, tiled=True)
    local, x, o = local_part(rate, events, qkv, o, x)
    grads, terms = weight_terms(rate, events, got, local, qkv, o, x)
    summed = lax.psum_scatter(terms, "seq", scatter_dimension=1, tiled=True)

    give = give_part(grads, w)
    taken = lax.ppermute(give, "core", [(0, 1), (1, 0)])
    part = keep_part(grads, w, taken)
    part = add_x(lax.all_to_all(part, "x", 0, 0, tiled=True))
    input_grad = add_y(lax.all_to_all(part, "y", 0, 0, tiled=True))

    summed, input_grad = lax.optimization_barrier((summed, input_grad))
    square, summed = square_of(summed)
    square = lax.all_to_all(square, TENSOR, 0, 0, tiled=True)
    square = lax.all_to_all(sum_of(square), "seq", 0, 0, tiled=True)
    weight_grad = scaled(square, summed)
    return (input_grad, weight_grad.reshape(3, DH, D // N_SEQ).transpose(2, 0, 1))


def solution(mesh):
    fine = Mesh(mesh.devices.reshape(N_SEQ, NX, NY, NC), ("seq",) + TENSOR)
    return jax.shard_map(
        body,
        mesh=fine,
        in_specs=(P("seq", None), P(None, None, TENSOR), P("seq", TENSOR), P(TENSOR), P()),
        out_specs=(P(TENSOR, "seq"), P("seq", None, TENSOR)),
        check_vma=False,
    )
```

```python
import math

import jax
import jax.numpy as jnp
from jax import lax
from jax.experimental import pallas as pl
from jax.experimental.pallas import tpu as pltpu
from jax.sharding import Mesh, PartitionSpec as P

DH = 96
TOK = 192
D = 6144
N_SEQ = 12
NX, NY, NC = 4, 8, 2
N_TENSOR = NX * NY * NC
OUT_ROWS = D // N_TENSOR
HALF = D // NC
PER_X = HALF // NX
PARTS = 3 * DH
K_BLOCK = 1536
S_BLOCK = 1536
PACK_ROWS = 72
PACK_REST = 32
BIG = 60 << 20
MIDDLE = 50 << 20
SMALL = 8 << 20

DROP_LOGARITHM = 0.3
CLIP_RMS = 0.5
SCALE = DH ** (-0.5)
F32 = jnp.float32
BF16 = jnp.bfloat16
TENSOR = ("x", "y", "core")

NN = (((1,), (0,)), ((), ()))
NT = (((1,), (1,)), ((), ()))
TN = (((0,), (0,)), ((), ()))
TT = (((0,), (1,)), ((), ()))


def dot(a, b, dims):
    return lax.dot_general(a, b, dims, preferred_element_type=F32)


def split(a):
    high = a.astype(BF16)
    return high, (a - high.astype(F32)).astype(BF16)


def dot_wide_left(a, b, dims):
    high, low = split(a)
    return dot(high, b, dims) + dot(low, b, dims)


def dot_wide_right(a, b, dims):
    high, low = split(b)
    return dot(a, high, dims) + dot(a, low, dims)


def log_decay(rate, events, first, steps):
    seen = jnp.zeros(steps.shape, F32)
    for k in range(events.shape[0]):
        place = events[k] - first
        seen += jnp.where((steps >= place) & (place >= 0), 1.0, 0.0)
    return -(rate * (steps + 1).astype(F32) + DROP_LOGARITHM * seen)


def tail_and_head(rate, events, first):
    steps = lax.broadcasted_iota(jnp.int32, (1, TOK), 1)
    cumul = log_decay(rate, events, first, steps)
    total = log_decay(rate, events, first, jnp.full((1, 1), TOK - 1, jnp.int32))
    return jnp.exp(total - cumul), jnp.exp(cumul)


def pack(state):
    rest = [state[PACK_ROWS:, k * PACK_REST : (k + 1) * PACK_REST] for k in range(DH // PACK_REST)]
    return jnp.concatenate([state[:PACK_ROWS], jnp.concatenate(rest, axis=0)], axis=1)


def unpack(packed):
    rows = DH - PACK_ROWS
    rest = [packed[k * rows : (k + 1) * rows, DH:] for k in range(DH // PACK_REST)]
    return jnp.concatenate([packed[:, :DH], jnp.concatenate(rest, axis=1)], axis=0)


def columns(k, size):
    return pl.ds(k * size, size)


def fetch(pairs, sems):
    copies = [pltpu.make_async_copy(a, b, sems.at[k]) for k, (a, b) in enumerate(pairs)]
    for copy in copies:
        copy.start()
    return copies


def wait(copies):
    for copy in copies:
        copy.wait()


def project_kernel(
    rate_ref, events_ref, x_ref, w_ref, o_ref, qkv_ref, send_ref,
    x_buf, w_buf, o_buf, acc, sems, o_sem,
):
    copies = []
    for k in range(D // K_BLOCK):
        at = columns(k, K_BLOCK)
        pair = (
            pltpu.make_async_copy(x_ref.at[:, at], x_buf.at[:, at], sems.at[0, k]),
            pltpu.make_async_copy(w_ref.at[:, at], w_buf.at[:, at], sems.at[1, k]),
        )
        for copy in pair:
            copy.start()
        copies.append(pair)
    o_copy = fetch([(o_ref, o_buf)], o_sem)
    for k, pair in enumerate(copies):
        wait(pair)
        at = columns(k, K_BLOCK)
        term = dot(w_buf[:, at], x_buf[:, at], NT)
        if k == 0:
            acc[...] = term
        else:
            acc[...] += term

    me = lax.axis_index("seq")
    rate = rate_ref[0]
    query = (acc[:DH] * SCALE).astype(BF16)
    keys = acc[DH : 2 * DH].astype(BF16)
    values = acc[2 * DH :].astype(BF16)
    qkv_ref[0] = query
    qkv_ref[1] = keys
    qkv_ref[2] = values
    tail_w, head_w = tail_and_head(rate, events_ref, me * TOK)
    forward = pack(dot_wide_left(values.astype(F32) * tail_w, keys, NT))
    wait(o_copy)
    reverse = pack(dot_wide_left(query.astype(F32) * head_w, o_buf[...], NN))
    for d in range(N_SEQ):
        low = (jnp.minimum(me, d) + 1) * TOK
        high = jnp.maximum(me, d) * TOK
        count = jnp.float32(0.0)
        for k in range(events_ref.shape[0]):
            inside = (events_ref[k] >= low) & (events_ref[k] < high)
            count += jnp.where(inside, 1.0, 0.0)
        gap = jnp.maximum(high - low, 0).astype(F32)
        weight = jnp.exp(jnp.full((1, 128), -(rate * gap + DROP_LOGARITHM * count), F32))
        send_ref[d] = (jnp.where(d > me, forward, reverse) * weight).astype(BF16)


def local_kernel(rate_ref, events_ref, qkv_ref, o_ref, x_ref, grads_ref, x_buf, x_sem):
    x_copy = fetch([(x_ref, x_buf)], x_sem)
    first = lax.axis_index("seq") * TOK
    rate = rate_ref[0]
    row = lax.broadcasted_iota(jnp.int32, (TOK, 1), 0)
    column = lax.broadcasted_iota(jnp.int32, (1, TOK), 1)
    later = row >= column
    gap = log_decay(rate, events_ref, first, row) - log_decay(rate, events_ref, first, column)
    weight = jnp.where(later, jnp.exp(jnp.where(later, gap, 0.0)), 0.0)
    query, keys, values, out = qkv_ref[0], qkv_ref[1], qkv_ref[2], o_ref[...]
    scores = dot(query, keys, TN) * weight
    dscores = dot(out, values, NN) * weight
    grads_ref[:DH] = dot_wide_right(keys, dscores, NT)
    grads_ref[DH : 2 * DH] = dot_wide_right(query, dscores, NN)
    grads_ref[2 * DH :] = dot_wide_right(out, scores, TN)
    wait(x_copy)


def weight_kernel(
    rate_ref, events_ref, got_ref, local_ref, qkv_ref, o_ref, x_ref, grads_ref, terms_ref,
    terms_buf, sems,
):
    me = lax.axis_index("seq")
    tail_w, head_w = tail_and_head(rate_ref[0], events_ref, me * TOK)
    prefix = jnp.zeros((PACK_ROWS, 128), F32)
    suffix = jnp.zeros((PACK_ROWS, 128), F32)
    for j in range(N_SEQ):
        state = got_ref[j].astype(F32)
        prefix += jnp.where(j < me, state, 0.0)
        suffix += jnp.where(j > me, state, 0.0)
    prefix, suffix = unpack(prefix), unpack(suffix)
    dquery = local_ref[:DH] + head_w * dot_wide_left(prefix, o_ref[...], TT)
    dkey = local_ref[DH : 2 * DH] + tail_w * dot_wide_left(suffix, qkv_ref[2], NN)
    dvalue = local_ref[2 * DH :] + tail_w * dot_wide_left(suffix, qkv_ref[1], TN)
    grads_ref[:DH] = (dquery * SCALE).astype(BF16)
    grads_ref[DH : 2 * DH] = dkey.astype(BF16)
    grads_ref[2 * DH :] = dvalue.astype(BF16)

    grads = grads_ref[...]
    sent = []
    for k in range(D // S_BLOCK):
        at = columns(k, S_BLOCK)
        terms_buf[:, at] = dot(grads, x_ref[:, at], NN).astype(BF16)
        copy = pltpu.make_async_copy(terms_buf.at[:, at], terms_ref.at[:, at], sems.at[k])
        copy.start()
        sent.append(copy)
    wait(sent)


def fetch_w(w_ref, w_buf, sems):
    chunks = [columns(k, D // NX) for k in range(NX)]
    return fetch([(w_ref.at[:, at], w_buf.at[:, at]) for at in chunks], sems)


def core_columns(w_buf, k, c):
    starts = [k * (D // NX) + (y * NC + c) * OUT_ROWS for y in range(NY)]
    return jnp.concatenate([w_buf[:, at : at + OUT_ROWS] for at in starts], axis=1)


def give_kernel(grads_ref, w_ref, give_ref, w_buf, sems):
    core = lax.axis_index("core")
    grads = grads_ref[...]
    for k, copy in enumerate(fetch_w(w_ref, w_buf, sems)):
        wait([copy])
        for c in range(NC):

            @pl.when(core != c)
            def _():
                give_ref[k] = dot(grads, core_columns(w_buf, k, c), TN).astype(BF16)


def keep_kernel(grads_ref, w_ref, taken_ref, sum_ref, w_buf, sems):
    core = lax.axis_index("core")
    grads = grads_ref[...]
    for k, copy in enumerate(fetch_w(w_ref, w_buf, sems)):
        wait([copy])
        for c in range(NC):

            @pl.when(core == c)
            def _():
                mine = dot(grads, core_columns(w_buf, k, c), TN)
                sum_ref[k] = (mine + taken_ref[k].astype(F32)).astype(BF16)


def add_x_kernel(part_ref, out_ref):
    total = part_ref[0].astype(F32)
    for j in range(1, NX):
        total += part_ref[j].astype(F32)
    total = total.T.astype(BF16)
    for y in range(NY):
        out_ref[y] = total[y * OUT_ROWS : (y + 1) * OUT_ROWS]


def add_y_kernel(part_ref, out_ref):
    total = part_ref[0].astype(F32)
    for j in range(1, NY):
        total += part_ref[j].astype(F32)
    out_ref[...] = total.astype(BF16)


def square_kernel(summed_ref, out_ref, held_ref):
    held_ref[...] = summed_ref[...]
    summed = summed_ref[...].astype(F32)
    total = jnp.sum(jnp.sum(summed * summed, axis=0, keepdims=True), axis=1, keepdims=True)
    out_ref[...] = jnp.broadcast_to(total, out_ref.shape)


def sum_kernel(parts_ref, out_ref):
    total = jnp.sum(parts_ref[...], axis=0, keepdims=True)
    for j in range(N_SEQ):
        out_ref[j] = total


def scale_kernel(parts_ref, summed_ref, out_ref):
    square = parts_ref[0]
    for j in range(1, N_SEQ):
        square += parts_ref[j]
    square = square[:, :1]
    limit = CLIP_RMS * math.sqrt(D * PARTS * N_TENSOR)
    factor = jnp.minimum(1.0, limit * lax.rsqrt(square + 1e-06))
    out_ref[...] = (summed_ref[...].astype(F32) * factor).astype(BF16)


SMEM = pl.BlockSpec(memory_space=pltpu.SMEM)
VMEM = pl.BlockSpec(memory_space=pltpu.VMEM)
HBM = pl.BlockSpec(memory_space=pltpu.HBM)
DMA = pltpu.SemaphoreType.DMA


def shape_of(shape, dtype=BF16):
    return jax.ShapeDtypeStruct(shape, dtype)


def call(kernel, in_specs, out_specs, out_shape, cost, scratch=(), limit=BIG, **grid):
    flops, moved = cost
    return pl.pallas_call(
        kernel,
        in_specs=in_specs,
        out_specs=out_specs,
        out_shape=out_shape,
        scratch_shapes=list(scratch),
        compiler_params=pltpu.CompilerParams(vmem_limit_bytes=limit),
        cost_estimate=pl.CostEstimate(flops=flops, bytes_accessed=moved, transcendentals=0),
        **grid,
    )


def project(rate, events, x, w, o):
    return call(
        project_kernel,
        [SMEM, SMEM, HBM, HBM, HBM],
        [VMEM, VMEM],
        [shape_of((3, DH, TOK)), shape_of((N_SEQ, PACK_ROWS, 128))],
        (2 * TOK * D * PARTS, 2 * D * (TOK + PARTS)),
        [
            pltpu.VMEM((TOK, D), BF16),
            pltpu.VMEM((PARTS, D), BF16),
            pltpu.VMEM((TOK, DH), BF16),
            pltpu.VMEM((PARTS, TOK), F32),
            DMA((2, D // K_BLOCK)),
            DMA((1,)),
        ],
    )(rate, events, x, w, o)


def local_part(rate, events, qkv, o, x):
    return call(
        local_kernel,
        [SMEM, SMEM, VMEM, VMEM, HBM],
        [VMEM, VMEM],
        [shape_of((PARTS, TOK), F32), shape_of((TOK, D))],
        (20 * TOK * TOK * DH, 8 * TOK * PARTS + 2 * TOK * D),
        [DMA((1,))],
        limit=MIDDLE,
    )(rate, events, qkv, o, x)


def weight_terms(rate, events, got, local, qkv, o, x):
    return call(
        weight_kernel,
        [SMEM, SMEM, VMEM, VMEM, VMEM, VMEM, VMEM],
        [VMEM, HBM],
        [shape_of((PARTS, TOK)), shape_of((PARTS, D))],
        (2 * TOK * D * PARTS, 2 * D * (TOK + PARTS)),
        [
            pltpu.VMEM((PARTS, D), BF16),
            DMA((D // S_BLOCK,)),
        ],
        limit=MIDDLE,
    )(rate, events, got, local, qkv, o, x)


def give_part(grads, w):
    return call(
        give_kernel,
        [VMEM, HBM],
        VMEM,
        shape_of((NX, TOK, PER_X)),
        (TOK * D * PARTS, D * (TOK + PARTS)),
        [pltpu.VMEM((PARTS, D), BF16), DMA((NX,))],
        limit=MIDDLE,
    )(grads, w)


def keep_part(grads, w, taken):
    return call(
        keep_kernel,
        [VMEM, HBM, VMEM],
        VMEM,
        shape_of((NX, TOK, PER_X)),
        (TOK * D * PARTS, D * (2 * TOK + PARTS)),
        [pltpu.VMEM((PARTS, D), BF16), DMA((NX,))],
        limit=MIDDLE,
    )(grads, w, taken)


def add_x(parts):
    shape = (NY, OUT_ROWS, TOK)
    return call(
        add_x_kernel, [VMEM], VMEM, shape_of(shape), (4 * parts.size, 4 * parts.size), limit=SMALL
    )(parts)


def add_y(parts):
    shape = (OUT_ROWS, TOK)
    return call(
        add_y_kernel, [VMEM], VMEM, shape_of(shape), (parts.size, 2 * parts.size), limit=SMALL
    )(parts)


def square_of(summed):
    return call(
        square_kernel,
        [VMEM],
        [VMEM, VMEM],
        [shape_of((N_TENSOR, 128), F32), shape_of(summed.shape)],
        (2 * summed.size, 2 * summed.size),
        limit=SMALL,
    )(summed)


def sum_of(parts):
    return call(
        sum_kernel, [VMEM], VMEM, shape_of((N_SEQ, 1, 128), F32), (parts.size, 4 * parts.size), limit=SMALL
    )(parts)


def scaled(parts, summed):
    return call(
        scale_kernel,
        [VMEM, VMEM],
        VMEM,
        shape_of(summed.shape),
        (2 * summed.size, 4 * summed.size),
        limit=SMALL,
    )(parts, summed)


def body(layer_inputs, projection_matrices, result_sensitivity, channel_fading_rate, loss_events):
    x, o, rate, events = layer_inputs, result_sensitivity, channel_fading_rate, loss_events
    w = projection_matrices.transpose(1, 2, 0).reshape(PARTS, D)
    qkv, send = project(rate, events, x, w, o)
    got = lax.all_to_all(send, "seq", 0, 0, tiled=True)
    local, x = local_part(rate, events, qkv, o, x)
    grads, terms = weight_terms(rate, events, got, local, qkv, o, x)
    summed = lax.psum_scatter(terms, "seq", scatter_dimension=1, tiled=True)

    give = give_part(grads, w)
    taken = lax.ppermute(give, "core", [(0, 1), (1, 0)])
    part = keep_part(grads, w, taken)
    part = add_x(lax.all_to_all(part, "x", 0, 0, tiled=True))
    input_grad = add_y(lax.all_to_all(part, "y", 0, 0, tiled=True))

    summed, input_grad = lax.optimization_barrier((summed, input_grad))
    square, summed = square_of(summed)
    square = lax.all_to_all(square, TENSOR[::-1], 0, 0, tiled=True)
    square = lax.all_to_all(sum_of(square), "seq", 0, 0, tiled=True)
    weight_grad = scaled(square, summed)
    return (input_grad, weight_grad.reshape(3, DH, D // N_SEQ).transpose(2, 0, 1))


def solution(mesh):
    fine = Mesh(mesh.devices.reshape(N_SEQ, NX, NY, NC), ("seq",) + TENSOR)
    return jax.shard_map(
        body,
        mesh=fine,
        in_specs=(P("seq", None), P(None, None, TENSOR), P("seq", TENSOR), P(TENSOR), P()),
        out_specs=(P(TENSOR, "seq"), P("seq", None, TENSOR)),
        check_vma=False,
    )
```
